32 devices in a mesh: wide: 8 (over z, y), narrow: 4 (over x, core).
Axes of the slice: x: 2, y: 2, z: 4, core: 2. Of those that a mesh axis runs over, the one named last changes fastest.
Arguments:
- entry_factor: bfloat16 [288, 4, 64, 1024], P('wide', 'narrow'), may hold values from -6 to 6
- entry_panel: int32 [288, 4], P('wide', 'narrow'), may hold values from 0 to 1
- entry_target: int32 [288, 4], P('wide', 'narrow'), may hold values from 0 to 7, as said below
- entry_count: int32 [4, 8], P('narrow', 'wide'), may hold values from 1 to 36, 96 in all within a row
- panel_shared: bfloat16 [16, 64, 1024], P('wide', None, 'narrow'), may hold values from -0.1875 to 0.1875
- coupling: float32 [16, 64, 64], P('wide'), may hold values from -0.75 to 0.75
- probes: bfloat16 [32, 64, 1024], P('narrow'), may hold values from -6 to 6
Outputs:
- left_factor: float32 [32, 64, 1024], P('narrow', None, 'wide')
- right_factor: float32 [32, 64, 1024], P('narrow', None, 'wide')
The draws below stay inside these ranges and needn't reach their ends.
Inputs may be any that keep to these rules, and one draw needn't show every extreme that they name: `entry_panel`: the local panel of an entry of any slot, live or not. `entry_target`: the local target of an entry; every target has at least one live entry. `entry_count`: the live slots of one device; for every owner the counts over the 8 wide indices sum to 96, and some device holds exactly 36.
All inputs are finite; a program needn't handle non-finite values.
Results may differ from the reference program's by a relative error of at most 0.0036.
Values may be sent and summed in bfloat16 or wider, within the bound.
A program may use at most 64 MiB of HBM per device.

```python
import math
import jax
import jax.numpy as jnp
import numpy as np
from jax import lax

B = 1024
R = 64
TGT_DEV = 8
DESC_DEV = 2
ENT_MEAN = 12
LIST_DEV = 36
OWNERS = 4
GROUPS = 8
TGT = 32
PANELS = 16
ENTRIES = 288
N_WIDE = 8


def draw_entry_target(key, part):
    row_index = jnp.arange(ENTRIES, dtype=jnp.int32)[:, None]
    owner_index = jnp.arange(OWNERS, dtype=jnp.int32)[None, :]
    random_target = jax.random.randint(key, (ENTRIES, OWNERS), 0, TGT_DEV, dtype=jnp.int32)
    first_target = (row_index // LIST_DEV + owner_index) % TGT_DEV
    return jnp.where(row_index % LIST_DEV == 0, first_target, random_target).astype(jnp.int32)


def touch_ends(drawn, rng, least, high):
    shape = drawn.shape
    index_at = [jax.random.randint(jax.random.fold_in(rng, axis), (), 0, shape[axis]) for axis in range(len(shape))]
    drawn = drawn.at[tuple(index_at)].set(least)
    longest = shape.index(max(shape))
    index_at[longest] = (index_at[longest] + 1) % shape[longest]
    return drawn.at[tuple(index_at)].set(high)


def steps_of(own_key, shape, cuts, least, largest):
    level = 1.0
    for axis_at, blocks in cuts:
        draws = jax.random.uniform(jax.random.fold_in(jax.random.fold_in(own_key, 6), axis_at), (blocks,), jnp.float32, least / len(cuts), largest / len(cuts))
        level = level * jnp.repeat(jnp.exp(draws), shape[axis_at] // blocks).reshape((-1,) + (1,) * (len(shape) - 1 - axis_at))
    return level


def length_profile(count, total, bound, lean):
    loads = [(1 << 20) // math.isqrt(standing ** lean) + 1 for standing in range(2, count + 1)]
    rest, given = total - bound - (count - 1), [1] * (count - 1)
    while rest > 0:
        free = [i for i in range(count - 1) if given[i] < bound]
        whole, left = sum([loads[i] for i in free]), rest
        for i in free:
            addition = min(bound - given[i], max(1, left * loads[i] // whole), rest)
            given[i] = given[i] + addition
            rest = rest - addition
    return np.array([bound] + given)


def ragged_sizes(own_key, number_of, total, bound, lean):
    if number_of == 2:
        one = jax.random.randint(own_key, (), max(1, total - bound), min(bound, total - 1) + 1)
        return jnp.stack([one, total - one])
    tallies = jnp.asarray(length_profile(number_of, total, bound, lean), jnp.int32)
    pairs = (number_of - 1) // 2
    giver, taker = tallies[1:1 + 2 * pairs:2], tallies[2:2 + 2 * pairs:2]
    margin = jnp.minimum(giver - 1, bound - taker)
    moved = jax.random.randint(jax.random.fold_in(own_key, 1), (pairs,), 0, 1 << 20) % (margin + 1)
    tallies = tallies.at[1:1 + 2 * pairs:2].set(giver - moved).at[2:2 + 2 * pairs:2].set(taker + moved)
    return tallies[jax.random.permutation(jax.random.fold_in(own_key, 2), number_of)]


def centred(stream_key, extent, scale, reach, shards=(), kind=jnp.bfloat16):
    array = jax.random.normal(stream_key, extent, jnp.float32) * scale
    if len(shards) > 0:
        array = steps_of(stream_key, extent, shards, -0.22, 0.18) * array
    return jnp.clip(array, min=-reach, max=reach).astype(kind)


def setup_inputs(seed: int = 0) -> dict:
    seeds = jax.random.split(jax.random.key(seed), 8)
    return {
        "entry_factor": centred(seeds[0], (ENTRIES, OWNERS, R, B), 1.0, 6.0, ((0, 8), (1, 4))),
        "entry_panel": touch_ends(jax.random.randint(seeds[1], (ENTRIES, OWNERS), 0, DESC_DEV), jax.random.fold_in(seeds[1], 1), 0, DESC_DEV - 1).astype(jnp.int32),
        "entry_target": draw_entry_target(jax.random.fold_in(seeds[7], 71), 0),
        "entry_count": jax.vmap(lambda own: ragged_sizes(own, GROUPS, ENT_MEAN * N_WIDE, LIST_DEV, 2))(jax.random.split(seeds[3], OWNERS)).reshape((OWNERS, GROUPS)).astype(jnp.int32),
        "panel_shared": centred(seeds[4], (PANELS, R, B), B ** -0.5, 0.1875, ((0, 8), (2, 4))),
        "coupling": centred(seeds[5], (PANELS, R, R), R ** -0.5, 0.75, ((0, 8),), jnp.float32),
        "probes": centred(seeds[6], (TGT, R, B), 1.0, 6.0, ((0, 4),)),
    }


def rounded(value):
    return lax.optimization_barrier(value.astype(jnp.bfloat16)).astype(jnp.float32)

def reference(entry_factor, entry_panel, entry_target, entry_count, panel_shared, coupling, probes):
    highest = lax.Precision.HIGHEST
    owner_count = entry_factor.shape[1]
    rank_dim = entry_factor.shape[2]
    full_width = entry_factor.shape[3]
    slot_ids = jnp.arange(LIST_DEV, dtype=jnp.int32)
    panel_ids = jnp.arange(DESC_DEV, dtype=jnp.int32)
    target_ids = jnp.arange(TGT_DEV, dtype=jnp.int32)
    probe_blocks = probes.astype(jnp.float32).reshape(owner_count, TGT_DEV, rank_dim, full_width)

    def group_data(group_index):
        entry_start = (group_index * LIST_DEV).astype(jnp.int32)
        factors = lax.dynamic_slice_in_dim(entry_factor, entry_start, LIST_DEV, 0).astype(jnp.float32)
        panels = lax.dynamic_slice_in_dim(entry_panel, entry_start, LIST_DEV, 0)
        targets = lax.dynamic_slice_in_dim(entry_target, entry_start, LIST_DEV, 0)
        counts = lax.dynamic_index_in_dim(entry_count, group_index, 1, keepdims=False)
        live_mask = (slot_ids[:, None] < counts[None, :]).astype(jnp.float32)
        pick_panel = (panels[:, :, None] == panel_ids[None, None, :]).astype(jnp.float32) * live_mask[:, :, None]
        pick_target = (targets[:, :, None] == target_ids[None, None, :]).astype(jnp.float32)
        panel_start = (group_index * DESC_DEV).astype(jnp.int32)
        shared = lax.dynamic_slice_in_dim(panel_shared, panel_start, DESC_DEV, 0).astype(jnp.float32)
        middle = lax.dynamic_slice_in_dim(coupling, panel_start, DESC_DEV, 0).astype(jnp.float32)
        return (factors, pick_panel, pick_target, shared, middle)

    def first_pass(sketch, group_index):
        factors, pick_panel, pick_target, shared, middle = group_data(group_index)
        projected = jnp.einsum('drb,otkb->dotrk', shared, probe_blocks, precision=highest)
        coefficients = rounded(jnp.einsum('dij,dotjk->dotik', middle, projected, precision=highest))
        weights = jnp.einsum('lod,lot->lodt', pick_panel, pick_target)
        chosen = jnp.einsum('lodt,dotik->loik', weights, coefficients, precision=highest)
        contributions = jnp.einsum('loji,lojb->loib', chosen, factors, precision=highest)
        return (sketch + jnp.einsum('lot,loib->otib', pick_target, contributions, precision=highest), None)
    zeros = jnp.zeros((owner_count, TGT_DEV, rank_dim, full_width), jnp.float32)
    group_list = jnp.arange(GROUPS, dtype=jnp.int32)
    sketch, _ = lax.scan(first_pass, zeros, group_list)
    gram_matrix = jnp.einsum('otib,otjb->otij', sketch, sketch, precision=highest)
    lower_factor = jnp.linalg.cholesky(gram_matrix)
    basis = lax.linalg.triangular_solve(lower_factor, sketch, left_side=True, lower=True)
    basis_round = rounded(basis)

    def second_pass(coeff_rows, group_index):
        factors, pick_panel, pick_target, shared, middle = group_data(group_index)
        selected = jnp.einsum('lot,otkb->lokb', pick_target, basis_round, precision=highest)
        back_terms = jnp.einsum('loib,lokb->loik', factors, selected, precision=highest)
        weights = jnp.einsum('lod,lot->lodt', pick_panel, pick_target)
        summed = jnp.einsum('lodt,loik->dotik', weights, back_terms, precision=highest)
        middle_terms = jnp.einsum('dotik,dij->dotkj', summed, middle, precision=highest)
        return (coeff_rows + jnp.einsum('dotkj,djb->otkb', middle_terms, shared, precision=highest), None)
    coeff_rows, _ = lax.scan(second_pass, zeros, group_list)
    root_width = math.sqrt(full_width)
    left_factor = (basis * root_width).reshape(TGT, rank_dim, full_width)
    right_factor = (coeff_rows / root_width).reshape(TGT, rank_dim, full_width)
    return (left_factor, right_factor)
```

```python
import functools
import math

import jax
import jax.numpy as jnp
from jax import lax
from jax.experimental import pallas as pl
from jax.experimental.pallas import tpu as pltpu
from jax.sharding import PartitionSpec as P

HIGHEST = lax.Precision.HIGHEST
LAST_DIMS = (((1,), (1,)), ((), ()))
ZWAY = 4
YWAY = 2
WAYS = ZWAY * YWAY
NARROW = 4
FSPLIT = 4

def wide_reduce(x, count):
    lead, rows, width = x.shape
    pieces = x.reshape(lead, rows, count, width // count).transpose(2, 0, 1, 3)
    pieces = lax.all_to_all(pieces, "wide", 0, 0, tiled=True)
    return pieces.sum(axis=0)


def wide_gather(x, count):
    lead, rows, width = x.shape
    copies = jnp.broadcast_to(x[None], (count, lead, rows, width))
    copies = lax.all_to_all(copies, "wide", 0, 0, tiled=True)
    return copies.transpose(1, 2, 0, 3).reshape(lead, rows, count * width)


def lower_inverse(lower):
    highest = lax.Precision.HIGHEST
    size = lower.shape[-1]
    eye = jnp.eye(size, dtype=lower.dtype)
    diag = jnp.diagonal(lower, axis1=-2, axis2=-1)
    strict = eye - lower / diag[..., :, None]
    unit_inverse = eye + strict
    power = strict
    for _ in range(max(size - 1, 1).bit_length() - 1):
        power = jnp.einsum("tij,tjk->tik", power, power, precision=highest)
        unit_inverse = unit_inverse + jnp.einsum(
            "tij,tjk->tik", unit_inverse, power, precision=highest
        )
    return unit_inverse / diag[..., None, :]


def shards(entry_factor, entry_panel, entry_target, entry_count, panel_shared, coupling, probes):
    highest = lax.Precision.HIGHEST
    factors = entry_factor[:, 0]
    slot_count = factors.shape[0]
    rank_dim = factors.shape[1]
    full_width = factors.shape[2]
    panel_count = panel_shared.shape[0]
    target_count = probes.shape[0]
    live_mask = (jnp.arange(slot_count) < entry_count[0, 0]).astype(jnp.float32)
    pick_panel = (entry_panel == jnp.arange(panel_count)[None, :]).astype(jnp.float32) * live_mask[
        :, None
    ]
    pick_target = (entry_target == jnp.arange(target_count)[None, :]).astype(jnp.float32)
    pair_pick = (pick_panel[:, :, None] * pick_target[:, None, :]).reshape(
        slot_count, panel_count * target_count
    )
    gathered = lax.all_gather(panel_shared, "narrow", axis=2, tiled=True)
    projected = jnp.einsum("drb,tkb->dtrk", gathered, probes, preferred_element_type=jnp.float32)
    coefficients = jnp.einsum("dij,dtjk->dtik", coupling, projected, precision=highest).astype(
        jnp.bfloat16
    )
    coeff_table = coefficients.reshape(panel_count * target_count, rank_dim * rank_dim)
    chosen = jnp.dot(
        pair_pick.astype(jnp.bfloat16), coeff_table, preferred_element_type=jnp.float32
    )
    chosen = chosen.astype(jnp.bfloat16).reshape(slot_count, rank_dim, rank_dim)
    contributions = jnp.einsum("eji,ejb->eib", chosen, factors, preferred_element_type=jnp.float32)
    sketch = jnp.einsum("et,eib->tib", pick_target, contributions, precision=highest)
    wide_count = lax.axis_size("wide")
    share_cols = full_width // wide_count
    sketch_own = wide_reduce(sketch, wide_count)
    gram_part = jnp.einsum("tib,tjb->tij", sketch_own, sketch_own, precision=highest)
    gram_copies = jnp.broadcast_to(gram_part[None], (wide_count,) + gram_part.shape)
    gram_matrix = lax.all_to_all(gram_copies, "wide", 0, 0, tiled=True).sum(axis=0)
    sketch_sum = wide_gather(sketch_own, wide_count)
    lower_factor = jnp.linalg.cholesky(gram_matrix)
    basis = jnp.einsum(
        "tij,tjb->tib", lower_inverse(lower_factor), sketch_sum, precision=highest
    )
    basis_round = basis.astype(jnp.bfloat16)
    own_basis = lax.dynamic_slice_in_dim(basis, lax.axis_index("wide") * share_cols, share_cols, 2)
    selected = jnp.einsum(
        "et,tkb->ekb",
        pick_target.astype(jnp.bfloat16),
        basis_round,
        preferred_element_type=jnp.float32,
    )
    selected = selected.astype(jnp.bfloat16)
    back_terms = jnp.einsum("eib,ekb->eik", factors, selected, preferred_element_type=jnp.float32)
    summed = jnp.einsum("ep,eik->pik", pair_pick, back_terms, precision=highest)
    summed = summed.reshape(panel_count, target_count, rank_dim, rank_dim)
    middle_terms = jnp.einsum("dtik,dij->dtkj", summed, coupling, precision=highest)
    partial_rows = jnp.einsum(
        "dtkj,djb->tkb", middle_terms, gathered.astype(jnp.float32), precision=highest
    )
    coeff_part = wide_reduce(partial_rows, wide_count)
    root_width = math.sqrt(full_width)
    return (own_basis * root_width, coeff_part / root_width)


def eliminate(gram):
    size = gram.shape[0]
    lane = lax.broadcasted_iota(jnp.int32, (size, size), 1)
    line = lax.broadcasted_iota(jnp.int32, (size, size), 0)
    eye = jnp.where(lane == line, 1.0, 0.0).astype(jnp.float32)
    whole = jnp.concatenate([gram, eye], axis=1)
    groups = [whole[8 * r : 8 * r + 8] for r in range(size // 8)]
    sub = lax.broadcasted_iota(jnp.int32, (8, 1), 0)
    for j in range(size):
        top, at = j // 8, j % 8
        row = groups[top][at : at + 1]
        scaled = row * (1.0 / row[:, j : j + 1])
        for r in range(top, size // 8):
            if r == top and at == 7:
                continue
            factor = groups[r][:, j : j + 1]
            if r == top:
                factor = jnp.where(sub > at, factor, 0.0)
            groups[r] = groups[r] - factor * scaled
    whole = jnp.concatenate(groups, axis=0)
    pivots = jnp.sum(jnp.where(lane == line, whole[:, :size], 0.0), axis=1, keepdims=True)
    return whole[:, size:] * (1.0 / jnp.sqrt(pivots))


def recompress(
    meta, f_hbm, p_hbm, s_hbm, cbd, left, right,
    fbuf, cum, pbuf, sfull, scol, coef, part, ysend, yrecv, zsend, zrecv, total, qall, midall,
    loc_sem, s_send, s_recv, c_send, c_recv, y_sem, yr_sem, z_sem, zr_sem,
    q_send, q_recv, m_send, m_recv,
):
    slots = f_hbm.shape[0]
    rank = f_hbm.shape[2]
    width = f_hbm.shape[3]
    quarter = width // NARROW
    share = width // WAYS
    w = lax.axis_index("wide")
    n = lax.axis_index("narrow")
    z, y = w // YWAY, w % YWAY
    flip = w + 1 - 2 * y

    def zflip(m):
        return (z, z + 1 - 2 * (z % 2), (z + 2) % 4, 3 - z)[m]

    def remote(src, dst, send, recv, wide_at, narrow_at):
        return pltpu.make_async_remote_copy(
            src_ref=src, dst_ref=dst, send_sem=send, recv_sem=recv,
            device_id=(wide_at, narrow_at), device_id_type=pl.DeviceIdType.MESH,
        )

    step = slots // FSPLIT
    loads = [
        pltpu.make_async_copy(
            f_hbm.at[pl.ds(i * step, step)], fbuf.at[pl.ds(i * step, step)], loc_sem.at[i]
        )
        for i in range(FSPLIT)
    ]
    own_s = pltpu.make_async_copy(s_hbm, sfull.at[n], loc_sem.at[FSPLIT])
    load_p = pltpu.make_async_copy(p_hbm, pbuf, loc_sem.at[FSPLIT + 1])
    own_s.start()
    for c in loads:
        c.start()
    load_p.start()

    barrier = pltpu.get_barrier_semaphore()
    for k in range(1, NARROW):
        pl.semaphore_signal(
            barrier, inc=1, device_id=(w, (n + k) % NARROW), device_id_type=pl.DeviceIdType.MESH
        )
    for k in range(1, WAYS):
        pl.semaphore_signal(
            barrier, inc=1, device_id=((w + k) % WAYS, n), device_id_type=pl.DeviceIdType.MESH
        )
    pl.semaphore_wait(barrier, NARROW + WAYS - 2)

    sent = []
    s_copies = []
    for k in range(1, NARROW):
        c = remote(s_hbm, sfull.at[n], s_send.at[k], s_recv.at[k], w, (n + k) % NARROW)
        c.start()
        sent.append(c)

    cum[slots] = jnp.zeros((2, rank, width), jnp.bfloat16)
    for c in loads:
        c.wait()
    for c0 in range(0, rank, 16):

        def add(s, acc):
            x = fbuf[meta[s], 0, pl.ds(c0, 16), :].astype(jnp.float32)
            acc = acc * meta[slots + s].astype(jnp.float32) + x
            high = acc.astype(jnp.bfloat16)
            cum[s, 0, pl.ds(c0, 16), :] = high
            cum[s, 1, pl.ds(c0, 16), :] = (acc - high.astype(jnp.float32)).astype(jnp.bfloat16)
            return acc

        lax.fori_loop(0, slots, add, jnp.zeros((16, width), jnp.float32), unroll=2)

    def pair_rows(t):
        first, second = meta[2 * slots + 2 * t], meta[2 * slots + 2 * t + 1]
        return jnp.concatenate(
            [cum[first, 0], cum[second, 0], cum[first, 1], cum[second, 1]], axis=0
        )

    load_p.wait()
    own_s.wait()

    def project(at):
        cols = pl.ds(pl.multiple_of(at * quarter, quarter), quarter)
        probe = pbuf[:, :, cols].reshape(-1, quarter)
        return lax.dot_general(
            probe, sfull[at], LAST_DIMS, preferred_element_type=jnp.float32
        )

    projected = project(n)
    for k in range(1, NARROW):
        at = (n + NARROW - k) % NARROW
        remote(s_hbm, sfull.at[at], s_send.at[k], s_recv.at[k], w, n).wait_recv()
        projected = projected + project(at)
    for k in range(1, WAYS):
        to = (w + k) % WAYS
        src = sfull.at[to // 2, :, pl.ds(pl.multiple_of((to % 2) * share, share), share)]
        c = remote(src, scol.at[w], c_send.at[k], c_recv.at[k], to, n)
        c.start()
        sent.append(c)
    scol[w] = sfull[w // 2, :, pl.ds(pl.multiple_of((w % 2) * share, share), share)]
    coef[...] = lax.dot_general(
        projected, cbd[...], LAST_DIMS, precision=HIGHEST, preferred_element_type=jnp.float32
    ).astype(jnp.bfloat16)

    def partial_sketch(t):
        lhs = coef[pl.ds(pl.multiple_of(t * rank, rank), rank), :]
        lhs = jnp.concatenate([lhs, lhs], axis=1)
        return jnp.dot(lhs, pair_rows(t), preferred_element_type=jnp.float32)

    order = (3, 2, 1, 0)
    y_copies = []
    for k, m in enumerate(order):
        ysend[k] = partial_sketch(zflip(m) * YWAY + (1 - y)).astype(jnp.bfloat16)
        c = remote(ysend.at[k], yrecv.at[k], y_sem.at[k], yr_sem.at[k], flip, n)
        c.start()
        sent.append(c)
        y_copies.append(c)
    for k, m in enumerate(order):
        part[k] = partial_sketch(zflip(m) * YWAY + y)
    z_copies = []
    for k, m in enumerate(order):
        y_copies[k].wait_recv()
        summed = part[k] + yrecv[k].astype(jnp.float32)
        if m:
            zsend[k] = summed.astype(jnp.bfloat16)
            c = remote(
                zsend.at[k], zrecv.at[k], z_sem.at[k], zr_sem.at[k], zflip(m) * YWAY + y, n
            )
            c.start()
            sent.append(c)
            z_copies.append(c)
        else:
            total[...] = summed
    for k in range(3):
        z_copies[k].wait_recv()
        total[...] += zrecv[k].astype(jnp.float32)

    sketch = total[...]
    gram = lax.dot_general(
        sketch, sketch, LAST_DIMS, precision=HIGHEST, preferred_element_type=jnp.float32
    )
    inverse = eliminate(gram)
    qall[w] = jnp.dot(
        inverse, sketch, precision=HIGHEST, preferred_element_type=jnp.float32
    ).astype(jnp.bfloat16)

    q_copies = {}
    for m in (3, 2, 1):
        c = remote(qall.at[w], qall.at[w], q_send.at[m], q_recv.at[m], zflip(m) * YWAY + y, n)
        c.start()
        sent.append(c)
    c = remote(qall.at[w], qall.at[w], q_send.at[0], q_recv.at[4], flip, n)
    c.start()
    sent.append(c)

    def middle(t):
        terms = lax.dot_general(
            qall[t], pair_rows(t), LAST_DIMS, preferred_element_type=jnp.float32
        )
        terms = terms[:, : 2 * rank] + terms[:, 2 * rank :]
        rows = jnp.dot(terms, cbd[...], precision=HIGHEST, preferred_element_type=jnp.float32)
        midall[w, pl.ds(pl.multiple_of(t * rank, rank), rank), :] = rows.astype(jnp.bfloat16)

    def q_wait(src, sem):
        remote(qall.at[w], qall.at[src], q_send.at[0], q_recv.at[sem], w, n).wait_recv()

    def mid_piece(src, m):
        first = zflip(m) * YWAY * rank
        return midall.at[src, pl.ds(pl.multiple_of(first, YWAY * rank), YWAY * rank), :]

    for m in range(ZWAY):
        near = zflip(m) * YWAY + y
        if m:
            q_wait(near, m)
            c = remote(qall.at[near], qall.at[near], q_send.at[4 + m], q_recv.at[4 + m], flip, n)
            c.start()
            sent.append(c)
        middle(near)
        far = zflip(m) * YWAY + 1 - y
        q_wait(far, 4 + m)
        middle(far)
        piece = mid_piece(w, m)
        for d in (3, 2, 1):
            c = remote(
                piece, piece, m_send.at[m, d], m_recv.at[m, d], zflip(d) * YWAY + y, n
            )
            c.start()
            sent.append(c)
        c = remote(piece, piece, m_send.at[m, 0], m_recv.at[m, 4], flip, n)
        c.start()
        sent.append(c)

    def mid_wait(src, m, d, sem):
        piece = mid_piece(src, m ^ d)
        remote(piece, piece, m_send.at[0, 0], m_recv.at[m, sem], w, n).wait_recv()
        return piece

    for m in range(ZWAY):
        for d in range(1, ZWAY):
            piece = mid_wait(zflip(d) * YWAY + y, m, d, d)
            c = remote(piece, piece, m_send.at[m, 4 + d], m_recv.at[m, 4 + d], flip, n)
            c.start()
            sent.append(c)

    for k in range(WAYS):
        cols = pl.ds(pl.multiple_of(w * share, share), share)
        left[k] = qall[k, :, cols]

    def rows_of(src):
        return jnp.dot(midall[src], scol[src], preferred_element_type=jnp.float32)

    for k in range(1, WAYS):
        src = (w + WAYS - k) % WAYS
        remote(scol.at[src], scol.at[src], c_send.at[k], c_recv.at[k], w, n).wait_recv()
    rows = rows_of(w)
    for d in range(1, ZWAY):
        rows = rows + rows_of(zflip(d) * YWAY + y)
    for d in range(ZWAY):
        src = zflip(d) * YWAY + 1 - y
        for m in range(ZWAY):
            mid_wait(src, m, d, 4 + d)
        rows = rows + rows_of(src)
    right[...] = rows.reshape(right.shape)
    for c in sent:
        c.wait_send()


def fused(entry_factor, entry_panel, entry_target, entry_count, panel_shared, coupling, probes):
    slots, _, rank, width = entry_factor.shape
    panels = panel_shared.shape[0]
    targets = probes.shape[0]
    pairs = targets * panels
    share = width // WAYS
    index = jnp.arange(slots, dtype=jnp.int32)
    key = jnp.where(
        index < entry_count[0, 0], entry_target[:, 0] * panels + entry_panel[:, 0], pairs
    )
    ahead = (key[None, :] < key[:, None]) | (
        (key[None, :] == key[:, None]) & (index[None, :] < index[:, None])
    )
    place = jnp.sum(ahead.astype(jnp.int32), axis=1)
    at = (place[None, :] == index[:, None]).astype(jnp.int32)
    order = jnp.sum(at * index[None, :], axis=1)
    sorted_key = jnp.sum(at * key[None, :], axis=1)
    before = jnp.sum((place[None, :] + 1 == index[:, None]) * (key[None, :] + 1), axis=1) - 1
    keep = (sorted_key == before).astype(jnp.int32)
    pair = jnp.arange(pairs, dtype=jnp.int32)
    upto = jnp.sum((key[None, :] <= pair[:, None]).astype(jnp.int32), axis=1)
    some = jnp.any(key[None, :] == pair[:, None], axis=1)
    meta = jnp.concatenate([order, keep, jnp.where(some, upto - 1, slots)])
    empty = jnp.zeros((rank, rank), jnp.float32)
    cbd = jnp.concatenate(
        [
            jnp.concatenate([coupling[0], empty], axis=1),
            jnp.concatenate([empty, coupling[1]], axis=1),
        ],
        axis=0,
    )
    depth = panels * rank
    bf16, f32 = jnp.bfloat16, jnp.float32
    dma = pltpu.SemaphoreType.DMA
    left, right = pl.pallas_call(
        recompress,
        out_shape=(
            jax.ShapeDtypeStruct((targets, rank, share), bf16),
            jax.ShapeDtypeStruct((targets, rank, share), f32),
        ),
        in_specs=[
            pl.BlockSpec(memory_space=pltpu.SMEM),
            pl.BlockSpec(memory_space=pl.ANY),
            pl.BlockSpec(memory_space=pl.ANY),
            pl.BlockSpec(memory_space=pl.ANY),
            pl.BlockSpec(memory_space=pltpu.VMEM),
        ],
        out_specs=(
            pl.BlockSpec(memory_space=pltpu.VMEM),
            pl.BlockSpec(memory_space=pltpu.VMEM),
        ),
        scratch_shapes=[
            pltpu.VMEM((slots, 1, rank, width), bf16),
            pltpu.VMEM((slots + 1, 2, rank, width), bf16),
            pltpu.VMEM((targets, rank, width), bf16),
            pltpu.VMEM((NARROW, depth, width // NARROW), bf16),
            pltpu.VMEM((WAYS, depth, share), bf16),
            pltpu.VMEM((targets * rank, depth), bf16),
            pltpu.VMEM((ZWAY, rank, width), f32),
            pltpu.VMEM((ZWAY, rank, width), bf16),
            pltpu.VMEM((ZWAY, rank, width), bf16),
            pltpu.VMEM((ZWAY - 1, rank, width), bf16),
            pltpu.VMEM((ZWAY - 1, rank, width), bf16),
            pltpu.VMEM((rank, width), f32),
            pltpu.VMEM((targets, rank, width), bf16),
            pltpu.VMEM((WAYS, targets * rank, depth), bf16),
            dma((FSPLIT + 2,)),
            dma((NARROW,)),
            dma((NARROW,)),
            dma((WAYS,)),
            dma((WAYS,)),
            dma((ZWAY,)),
            dma((ZWAY,)),
            dma((ZWAY,)),
            dma((ZWAY,)),
            dma((WAYS,)),
            dma((WAYS,)),
            dma((ZWAY, WAYS)),
            dma((ZWAY, WAYS)),
        ],
        compiler_params=pltpu.CompilerParams(
            collective_id=0, has_side_effects=True, vmem_limit_bytes=48 * 1024 * 1024
        ),
        name="recompress",
    )(meta, entry_factor, probes, panel_shared.reshape(depth, width // NARROW), cbd)
    root_width = math.sqrt(width)
    return (left.astype(f32) * root_width, right / root_width)


def solution(mesh):
    placed = (
        P("wide", "narrow", None, None),
        P("wide", "narrow"),
        P("wide", "narrow"),
        P("narrow", "wide"),
        P("wide", None, "narrow"),
        P("wide", None, None),
        P("narrow", None, None),
    )
    return jax.shard_map(
        fused if mesh.shape["wide"] == WAYS and mesh.shape["narrow"] == NARROW else shards,
        mesh=mesh,
        in_specs=placed,
        out_specs=(P("narrow", None, "wide"), P("narrow", None, "wide")),
        check_vma=False,
    )
```

```python
import functools
import math

import jax
import jax.numpy as jnp
from jax import lax
from jax.experimental import pallas as pl
from jax.experimental.pallas import tpu as pltpu
from jax.sharding import PartitionSpec as P

HIGHEST = lax.Precision.HIGHEST
LAST_DIMS = (((1,), (1,)), ((), ()))
ZWAY = 4
YWAY = 2
WAYS = ZWAY * YWAY
NARROW = 4
FSPLIT = 4
RCUT = 2

def wide_reduce(x, count):
    lead, rows, width = x.shape
    pieces = x.reshape(lead, rows, count, width // count).transpose(2, 0, 1, 3)
    pieces = lax.all_to_all(pieces, "wide", 0, 0, tiled=True)
    return pieces.sum(axis=0)


def wide_gather(x, count):
    lead, rows, width = x.shape
    copies = jnp.broadcast_to(x[None], (count, lead, rows, width))
    copies = lax.all_to_all(copies, "wide", 0, 0, tiled=True)
    return copies.transpose(1, 2, 0, 3).reshape(lead, rows, count * width)


def lower_inverse(lower):
    highest = lax.Precision.HIGHEST
    size = lower.shape[-1]
    eye = jnp.eye(size, dtype=lower.dtype)
    diag = jnp.diagonal(lower, axis1=-2, axis2=-1)
    strict = eye - lower / diag[..., :, None]
    unit_inverse = eye + strict
    power = strict
    for _ in range(max(size - 1, 1).bit_length() - 1):
        power = jnp.einsum("tij,tjk->tik", power, power, precision=highest)
        unit_inverse = unit_inverse + jnp.einsum(
            "tij,tjk->tik", unit_inverse, power, precision=highest
        )
    return unit_inverse / diag[..., None, :]


def shards(entry_factor, entry_panel, entry_target, entry_count, panel_shared, coupling, probes):
    highest = lax.Precision.HIGHEST
    factors = entry_factor[:, 0]
    slot_count = factors.shape[0]
    rank_dim = factors.shape[1]
    full_width = factors.shape[2]
    panel_count = panel_shared.shape[0]
    target_count = probes.shape[0]
    live_mask = (jnp.arange(slot_count) < entry_count[0, 0]).astype(jnp.float32)
    pick_panel = (entry_panel == jnp.arange(panel_count)[None, :]).astype(jnp.float32) * live_mask[
        :, None
    ]
    pick_target = (entry_target == jnp.arange(target_count)[None, :]).astype(jnp.float32)
    pair_pick = (pick_panel[:, :, None] * pick_target[:, None, :]).reshape(
        slot_count, panel_count * target_count
    )
    gathered = lax.all_gather(panel_shared, "narrow", axis=2, tiled=True)
    projected = jnp.einsum("drb,tkb->dtrk", gathered, probes, preferred_element_type=jnp.float32)
    coefficients = jnp.einsum("dij,dtjk->dtik", coupling, projected, precision=highest).astype(
        jnp.bfloat16
    )
    coeff_table = coefficients.reshape(panel_count * target_count, rank_dim * rank_dim)
    chosen = jnp.dot(
        pair_pick.astype(jnp.bfloat16), coeff_table, preferred_element_type=jnp.float32
    )
    chosen = chosen.astype(jnp.bfloat16).reshape(slot_count, rank_dim, rank_dim)
    contributions = jnp.einsum("eji,ejb->eib", chosen, factors, preferred_element_type=jnp.float32)
    sketch = jnp.einsum("et,eib->tib", pick_target, contributions, precision=highest)
    wide_count = lax.axis_size("wide")
    share_cols = full_width // wide_count
    sketch_own = wide_reduce(sketch, wide_count)
    gram_part = jnp.einsum("tib,tjb->tij", sketch_own, sketch_own, precision=highest)
    gram_copies = jnp.broadcast_to(gram_part[None], (wide_count,) + gram_part.shape)
    gram_matrix = lax.all_to_all(gram_copies, "wide", 0, 0, tiled=True).sum(axis=0)
    sketch_sum = wide_gather(sketch_own, wide_count)
    lower_factor = jnp.linalg.cholesky(gram_matrix)
    basis = jnp.einsum(
        "tij,tjb->tib", lower_inverse(lower_factor), sketch_sum, precision=highest
    )
    basis_round = basis.astype(jnp.bfloat16)
    own_basis = lax.dynamic_slice_in_dim(basis, lax.axis_index("wide") * share_cols, share_cols, 2)
    selected = jnp.einsum(
        "et,tkb->ekb",
        pick_target.astype(jnp.bfloat16),
        basis_round,
        preferred_element_type=jnp.float32,
    )
    selected = selected.astype(jnp.bfloat16)
    back_terms = jnp.einsum("eib,ekb->eik", factors, selected, preferred_element_type=jnp.float32)
    summed = jnp.einsum("ep,eik->pik", pair_pick, back_terms, precision=highest)
    summed = summed.reshape(panel_count, target_count, rank_dim, rank_dim)
    middle_terms = jnp.einsum("dtik,dij->dtkj", summed, coupling, precision=highest)
    partial_rows = jnp.einsum(
        "dtkj,djb->tkb", middle_terms, gathered.astype(jnp.float32), precision=highest
    )
    coeff_part = wide_reduce(partial_rows, wide_count)
    root_width = math.sqrt(full_width)
    return (own_basis * root_width, coeff_part / root_width)


def eliminate(gram):
    size = gram.shape[0]
    lane = lax.broadcasted_iota(jnp.int32, (size, size), 1)
    line = lax.broadcasted_iota(jnp.int32, (size, size), 0)
    eye = jnp.where(lane == line, 1.0, 0.0).astype(jnp.float32)
    whole = jnp.concatenate([gram, eye], axis=1)
    groups = [whole[8 * r : 8 * r + 8] for r in range(size // 8)]
    sub = lax.broadcasted_iota(jnp.int32, (8, 1), 0)
    for j in range(size):
        top, at = j // 8, j % 8
        row = groups[top][at : at + 1]
        scaled = row * (1.0 / row[:, j : j + 1])
        for r in range(top, size // 8):
            if r == top and at == 7:
                continue
            factor = groups[r][:, j : j + 1]
            if r == top:
                factor = jnp.where(sub > at, factor, 0.0)
            groups[r] = groups[r] - factor * scaled
    whole = jnp.concatenate(groups, axis=0)
    pivots = jnp.sum(jnp.where(lane == line, whole[:, :size], 0.0), axis=1, keepdims=True)
    return whole[:, size:] * (1.0 / jnp.sqrt(pivots))


def entry_order(panel, target, count, panels):
    slots = panel.shape[1]
    shape = (slots, slots)
    lane = lax.broadcasted_iota(jnp.int32, shape, 1)
    line = lax.broadcasted_iota(jnp.int32, shape, 0)
    across = jnp.where(lane[:1] < count, target * panels + panel, slots * panels)
    key = jnp.sum(jnp.where(line == lane, across, 0), axis=1, keepdims=True)
    ahead = (across < key) | ((across == key) & (lane < line))
    place = jnp.sum(ahead.astype(jnp.int32), axis=1, keepdims=True)
    order = jnp.sum(jnp.where(place == lane, line, 0), axis=0, keepdims=True)
    here = jnp.sum(jnp.where(place == lane, key + 1, 0), axis=0, keepdims=True)
    before = jnp.sum(jnp.where(place + 1 == lane, key + 1, 0), axis=0, keepdims=True)
    keep = (here == before).astype(jnp.int32)
    upto = jnp.sum((key <= lane).astype(jnp.int32), axis=0, keepdims=True)
    some = jnp.sum((key == lane).astype(jnp.int32), axis=0, keepdims=True)
    last = jnp.where(some > 0, upto - 1, slots)
    return order, keep, last


def recompress(
    f_hbm, panel_hbm, target_hbm, count_hbm, s_hbm, c_hbm, p_hbm, left, right,
    panel, target, count, order_vec, meta, coup, cbd, fbuf, cum, pbuf, sfull, scol, coef, part, ysend, yrecv, zsend, zrecv, total, qall, midall,
    loc_sem, small_sem, s_send, s_recv, c_send, c_recv, y_sem, yr_sem, z_sem, zr_sem,
    q_send, q_recv, m_send, m_recv,
):
    slots = f_hbm.shape[0]
    rank = f_hbm.shape[2]
    width = f_hbm.shape[3]
    quarter = width // NARROW
    share = width // WAYS
    w = lax.axis_index("wide")
    n = lax.axis_index("narrow")
    z, y = w // YWAY, w % YWAY
    flip = w + 1 - 2 * y

    def zflip(m):
        return (z, z + 1 - 2 * (z % 2), (z + 2) % 4, 3 - z)[m]

    def remote(src, dst, send, recv, wide_at, narrow_at):
        return pltpu.make_async_remote_copy(
            src_ref=src, dst_ref=dst, send_sem=send, recv_sem=recv,
            device_id=(wide_at, narrow_at), device_id_type=pl.DeviceIdType.MESH,
        )

    smalls = [
        pltpu.make_async_copy(src, dst, small_sem.at[i])
        for i, (src, dst) in enumerate(
            ((panel_hbm, panel), (target_hbm, target), (count_hbm, count), (c_hbm, coup))
        )
    ]
    step = slots // FSPLIT
    loads = [
        pltpu.make_async_copy(
            f_hbm.at[pl.ds(i * step, step)], fbuf.at[pl.ds(i * step, step)], loc_sem.at[i]
        )
        for i in range(FSPLIT)
    ]
    own_s = pltpu.make_async_copy(s_hbm, sfull.at[n], loc_sem.at[FSPLIT])
    load_p = pltpu.make_async_copy(p_hbm, pbuf, loc_sem.at[FSPLIT + 1])
    for c in smalls:
        c.start()
    own_s.start()
    for c in loads:
        c.start()
    load_p.start()

    barrier = pltpu.get_barrier_semaphore()
    for k in range(1, NARROW):
        pl.semaphore_signal(
            barrier, inc=1, device_id=(w, (n + k) % NARROW), device_id_type=pl.DeviceIdType.MESH
        )
    for k in range(1, WAYS):
        pl.semaphore_signal(
            barrier, inc=1, device_id=((w + k) % WAYS, n), device_id_type=pl.DeviceIdType.MESH
        )
    for c in smalls:
        c.wait()
    order_vec[...] = jnp.zeros(order_vec.shape, jnp.int32)
    for i, row in enumerate(entry_order(panel[...], target[...], count[...], coup.shape[0])):
        order_vec[i : i + 1, :slots] = row
    meta_copy = pltpu.make_async_copy(order_vec, meta, small_sem.at[4])
    meta_copy.start()
    empty = jnp.zeros((rank, rank), jnp.float32)
    cbd[:rank] = jnp.concatenate([coup[0], empty], axis=1)
    cbd[rank:] = jnp.concatenate([empty, coup[1]], axis=1)
    pl.semaphore_wait(barrier, NARROW + WAYS - 2)

    sent = []
    s_copies = []
    for k in range(1, NARROW):
        c = remote(s_hbm, sfull.at[n], s_send.at[k], s_recv.at[k], w, (n + k) % NARROW)
        c.start()
        sent.append(c)

    cum[slots] = jnp.zeros((2, rank, width), jnp.bfloat16)
    meta_copy.wait()
    for c in loads:
        c.wait()
    for c0 in range(0, rank, 16):

        def add(s, acc):
            x = fbuf[meta[0, s], 0, pl.ds(c0, 16), :].astype(jnp.float32)
            acc = acc * meta[1, s].astype(jnp.float32) + x
            high = acc.astype(jnp.bfloat16)
            cum[s, 0, pl.ds(c0, 16), :] = high
            cum[s, 1, pl.ds(c0, 16), :] = (acc - high.astype(jnp.float32)).astype(jnp.bfloat16)
            return acc

        lax.fori_loop(0, slots, add, jnp.zeros((16, width), jnp.float32), unroll=2)

    def pair_rows(t):
        first, second = meta[2, 2 * t], meta[2, 2 * t + 1]
        return jnp.concatenate(
            [cum[first, 0], cum[second, 0], cum[first, 1], cum[second, 1]], axis=0
        )

    load_p.wait()
    own_s.wait()

    def project(at):
        cols = pl.ds(pl.multiple_of(at * quarter, quarter), quarter)
        probe = pbuf[:, :, cols].reshape(-1, quarter)
        return lax.dot_general(
            probe, sfull[at].reshape(-1, quarter), LAST_DIMS, preferred_element_type=jnp.float32
        )

    projected = project(n)
    for k in range(1, NARROW):
        at = (n + NARROW - k) % NARROW
        remote(s_hbm, sfull.at[at], s_send.at[k], s_recv.at[k], w, n).wait_recv()
        projected = projected + project(at)
    coef[...] = lax.dot_general(
        projected, cbd[...], LAST_DIMS, precision=HIGHEST, preferred_element_type=jnp.float32
    ).astype(jnp.bfloat16)

    def partial_sketch(t):
        lhs = coef[pl.ds(pl.multiple_of(t * rank, rank), rank), :]
        lhs = jnp.concatenate([lhs, lhs], axis=1)
        return jnp.dot(lhs, pair_rows(t), preferred_element_type=jnp.float32)

    order = (3, 2, 1, 0)
    cut = rank // RCUT
    y_copies, z_copies = {}, {}
    for k, m in enumerate(order):
        ysend[k] = partial_sketch(zflip(m) * YWAY + (1 - y)).astype(jnp.bfloat16)
        for h in range(RCUT):
            at = pl.ds(h * cut, cut)
            c = remote(
                ysend.at[k, at], yrecv.at[k, at], y_sem.at[k, h], yr_sem.at[k, h], flip, n
            )
            c.start()
            sent.append(c)
            y_copies[k, h] = c
    for k, m in enumerate(order):
        part[k] = partial_sketch(zflip(m) * YWAY + y)
    for k, m in enumerate(order):
        for h in range(RCUT):
            at = pl.ds(h * cut, cut)
            y_copies[k, h].wait_recv()
            summed = part[k, at] + yrecv[k, at].astype(jnp.float32)
            if m:
                zsend[k, at] = summed.astype(jnp.bfloat16)
                c = remote(
                    zsend.at[k, at], zrecv.at[k, at], z_sem.at[k, h], zr_sem.at[k, h],
                    zflip(m) * YWAY + y, n,
                )
                c.start()
                sent.append(c)
                z_copies[k, h] = c
            else:
                total[at] = summed
    for k in (2, 0, 1):
        for h in range(RCUT):
            at = pl.ds(h * cut, cut)
            z_copies[k, h].wait_recv()
            total[at] += zrecv[k, at].astype(jnp.float32)

    for k in range(1, WAYS):
        to = (w + k) % WAYS
        src = sfull.at[to // 2, :, :, pl.ds(pl.multiple_of((to % 2) * share, share), share)]
        c = remote(src, scol.at[w], c_send.at[k], c_recv.at[k], to, n)
        c.start()
        sent.append(c)
    scol[w] = sfull[w // 2, :, :, pl.ds(pl.multiple_of((w % 2) * share, share), share)]

    sketch = total[...]
    gram = lax.dot_general(
        sketch, sketch, LAST_DIMS, precision=HIGHEST, preferred_element_type=jnp.float32
    )
    inverse = eliminate(gram)
    qall[w] = jnp.dot(
        inverse, sketch, precision=HIGHEST, preferred_element_type=jnp.float32
    ).astype(jnp.bfloat16)

    def middle(t):
        terms = lax.dot_general(
            qall[t], pair_rows(t), LAST_DIMS, preferred_element_type=jnp.float32
        )
        terms = terms[:, : 2 * rank] + terms[:, 2 * rank :]
        rows = jnp.dot(terms, cbd[...], precision=HIGHEST, preferred_element_type=jnp.float32)
        midall[w, pl.ds(pl.multiple_of(t * rank, rank), rank), :] = rows.astype(jnp.bfloat16)

    def arrivals(at):
        return (at, at + 1 - 2 * (at % 2), 2 - at // 2, 3 - 3 * (at // 2))

    inner = z % 3 != 0
    later = []

    def start(c, holds=None):
        if holds is None:
            c.start()
        else:
            pl.when(holds)(c.start)
        later.append((c, holds))

    def spread(ref, send, recv):
        start(remote(ref, ref, send(1), recv(z), (z + 1) % 4 * YWAY + y, n), z < ZWAY - 1)
        start(remote(ref, ref, send(2), recv(z), (z + 3) % 4 * YWAY + y, n), z > 0)
        start(remote(ref, ref, send(0), recv(ZWAY + z), flip, n))

    def pass_on(ref, j, src_z, send, recv):
        remote(ref, ref, send(0), recv(src_z), w, n).wait_recv()
        to = (3 - z if j == 1 else (3 * z + 1) % 4) * YWAY + y
        start(remote(ref, ref, send(1 + 2 * j), recv(src_z), to, n), inner)
        start(remote(ref, ref, send(2 + 2 * j), recv(ZWAY + src_z), flip, n))

    def take(ref, src_z, send, recv):
        remote(ref, ref, send(0), recv(ZWAY + src_z), w, n).wait_recv()

    def q_sem(i):
        return q_send.at[i]

    def q_got(i):
        return q_recv.at[i]

    def mid_sems(i):
        return (lambda k: m_send.at[i, k]), (lambda k: m_recv.at[i, k])

    def mid_piece(src_z, src_y, i):
        first = arrivals(src_z)[i] * YWAY * rank
        rows = pl.ds(pl.multiple_of(first, YWAY * rank), YWAY * rank)
        return midall.at[src_z * YWAY + src_y, rows, :]

    spread(qall.at[w], q_sem, q_got)
    for j, src_z in enumerate(arrivals(z)):
        near, far = src_z * YWAY + y, src_z * YWAY + 1 - y
        if j:
            pass_on(qall.at[near], j, src_z, q_sem, q_got)
        middle(near)
        take(qall.at[far], src_z, q_sem, q_got)
        middle(far)
        spread(mid_piece(z, y, j), *mid_sems(j))

    for i in range(ZWAY):
        for j, src_z in enumerate(arrivals(z)):
            if j:
                pass_on(mid_piece(src_z, y, i), j, src_z, *mid_sems(i))

    for k in range(WAYS):
        cols = pl.ds(pl.multiple_of(w * share, share), share)
        left[k] = qall[k, :, cols]

    def rows_of(src):
        return jnp.dot(
            midall[src], scol[src].reshape(-1, share), preferred_element_type=jnp.float32
        )

    for k in range(1, WAYS):
        src = (w + WAYS - k) % WAYS
        remote(scol.at[src], scol.at[src], c_send.at[k], c_recv.at[k], w, n).wait_recv()
    rows = rows_of(w)
    for j, src_z in enumerate(arrivals(z)):
        if j:
            rows = rows + rows_of(src_z * YWAY + y)
    for src_z in arrivals(z):
        for i in range(ZWAY):
            take(mid_piece(src_z, 1 - y, i), src_z, *mid_sems(i))
        rows = rows + rows_of(src_z * YWAY + 1 - y)
    right[...] = rows.reshape(right.shape)
    for c in sent:
        c.wait_send()
    for c, holds in later:
        if holds is None:
            c.wait_send()
        else:
            pl.when(holds)(c.wait_send)


def fused(entry_factor, entry_panel, entry_target, entry_count, panel_shared, coupling, probes):
    slots, _, rank, width = entry_factor.shape
    panels = panel_shared.shape[0]
    targets = probes.shape[0]
    share = width // WAYS
    depth = panels * rank
    bf16, f32, i32 = jnp.bfloat16, jnp.float32, jnp.int32
    dma = pltpu.SemaphoreType.DMA
    left, right = pl.pallas_call(
        recompress,
        out_shape=(
            jax.ShapeDtypeStruct((targets, rank, share), bf16),
            jax.ShapeDtypeStruct((targets, rank, share), f32),
        ),
        in_specs=[pl.BlockSpec(memory_space=pltpu.HBM)] * 7,
        out_specs=(
            pl.BlockSpec(memory_space=pltpu.VMEM),
            pl.BlockSpec(memory_space=pltpu.VMEM),
        ),
        scratch_shapes=[
            pltpu.VMEM((1, slots), i32),
            pltpu.VMEM((1, slots), i32),
            pltpu.VMEM((1, 1), i32),
            pltpu.VMEM((8, 128), i32),
            pltpu.SMEM((8, 128), i32),
            pltpu.VMEM((panels, rank, rank), f32),
            pltpu.VMEM((depth, depth), f32),
            pltpu.VMEM((slots, 1, rank, width), bf16),
            pltpu.VMEM((slots + 1, 2, rank, width), bf16),
            pltpu.VMEM((targets, rank, width), bf16),
            pltpu.VMEM((NARROW, panels, rank, width // NARROW), bf16),
            pltpu.VMEM((WAYS, panels, rank, share), bf16),
            pltpu.VMEM((targets * rank, depth), bf16),
            pltpu.VMEM((ZWAY, rank, width), f32),
            pltpu.VMEM((ZWAY, rank, width), bf16),
            pltpu.VMEM((ZWAY, rank, width), bf16),
            pltpu.VMEM((ZWAY - 1, rank, width), bf16),
            pltpu.VMEM((ZWAY - 1, rank, width), bf16),
            pltpu.VMEM((rank, width), f32),
            pltpu.VMEM((targets, rank, width), bf16),
            pltpu.VMEM((WAYS, targets * rank, depth), bf16),
            dma((FSPLIT + 2,)),
            dma((5,)),
            dma((NARROW,)),
            dma((NARROW,)),
            dma((WAYS,)),
            dma((WAYS,)),
            dma((ZWAY, RCUT)),
            dma((ZWAY, RCUT)),
            dma((ZWAY, RCUT)),
            dma((ZWAY, RCUT)),
            dma((9,)),
            dma((WAYS,)),
            dma((ZWAY, 9)),
            dma((ZWAY, WAYS)),
        ],
        compiler_params=pltpu.CompilerParams(
            collective_id=0, has_side_effects=True, vmem_limit_bytes=63 * 1024 * 1024
        ),
        name="recompress",
    )(entry_factor, entry_panel.T, entry_target.T, entry_count, panel_shared, coupling, probes)
    root_width = math.sqrt(width)
    return (left.astype(f32) * root_width, right / root_width)


def solution(mesh):
    placed = (
        P("wide", "narrow", None, None),
        P("wide", "narrow"),
        P("wide", "narrow"),
        P("narrow", "wide"),
        P("wide", None, "narrow"),
        P("wide", None, None),
        P("narrow", None, None),
    )
    return jax.shard_map(
        fused if mesh.shape["wide"] == WAYS and mesh.shape["narrow"] == NARROW else shards,
        mesh=mesh,
        in_specs=placed,
        out_specs=(P("narrow", None, "wide"), P("narrow", None, "wide")),
        check_vma=False,
    )
```

```python
import functools
import math

import jax
import jax.numpy as jnp
from jax import lax
from jax.experimental import pallas as pl
from jax.experimental.pallas import tpu as pltpu
from jax.sharding import PartitionSpec as P

HIGHEST = lax.Precision.HIGHEST
LAST_DIMS = (((1,), (1,)), ((), ()))
ZWAY = 4
YWAY = 2
WAYS = ZWAY * YWAY
NARROW = 4
FSPLIT = 4
RCUT = 2
QCUT = 2

def wide_reduce(x, count):
    lead, rows, width = x.shape
    pieces = x.reshape(lead, rows, count, width // count).transpose(2, 0, 1, 3)
    pieces = lax.all_to_all(pieces, "wide", 0, 0, tiled=True)
    return pieces.sum(axis=0)


def wide_gather(x, count):
    lead, rows, width = x.shape
    copies = jnp.broadcast_to(x[None], (count, lead, rows, width))
    copies = lax.all_to_all(copies, "wide", 0, 0, tiled=True)
    return copies.transpose(1, 2, 0, 3).reshape(lead, rows, count * width)


def lower_inverse(lower):
    highest = lax.Precision.HIGHEST
    size = lower.shape[-1]
    eye = jnp.eye(size, dtype=lower.dtype)
    diag = jnp.diagonal(lower, axis1=-2, axis2=-1)
    strict = eye - lower / diag[..., :, None]
    unit_inverse = eye + strict
    power = strict
    for _ in range(max(size - 1, 1).bit_length() - 1):
        power = jnp.einsum("tij,tjk->tik", power, power, precision=highest)
        unit_inverse = unit_inverse + jnp.einsum(
            "tij,tjk->tik", unit_inverse, power, precision=highest
        )
    return unit_inverse / diag[..., None, :]


def shards(entry_factor, entry_panel, entry_target, entry_count, panel_shared, coupling, probes):
    highest = lax.Precision.HIGHEST
    factors = entry_factor[:, 0]
    slot_count = factors.shape[0]
    rank_dim = factors.shape[1]
    full_width = factors.shape[2]
    panel_count = panel_shared.shape[0]
    target_count = probes.shape[0]
    live_mask = (jnp.arange(slot_count) < entry_count[0, 0]).astype(jnp.float32)
    pick_panel = (entry_panel == jnp.arange(panel_count)[None, :]).astype(jnp.float32) * live_mask[
        :, None
    ]
    pick_target = (entry_target == jnp.arange(target_count)[None, :]).astype(jnp.float32)
    pair_pick = (pick_panel[:, :, None] * pick_target[:, None, :]).reshape(
        slot_count, panel_count * target_count
    )
    gathered = lax.all_gather(panel_shared, "narrow", axis=2, tiled=True)
    projected = jnp.einsum("drb,tkb->dtrk", gathered, probes, preferred_element_type=jnp.float32)
    coefficients = jnp.einsum("dij,dtjk->dtik", coupling, projected, precision=highest).astype(
        jnp.bfloat16
    )
    coeff_table = coefficients.reshape(panel_count * target_count, rank_dim * rank_dim)
    chosen = jnp.dot(
        pair_pick.astype(jnp.bfloat16), coeff_table, preferred_element_type=jnp.float32
    )
    chosen = chosen.astype(jnp.bfloat16).reshape(slot_count, rank_dim, rank_dim)
    contributions = jnp.einsum("eji,ejb->eib", chosen, factors, preferred_element_type=jnp.float32)
    sketch = jnp.einsum("et,eib->tib", pick_target, contributions, precision=highest)
    wide_count = lax.axis_size("wide")
    share_cols = full_width // wide_count
    sketch_own = wide_reduce(sketch, wide_count)
    gram_part = jnp.einsum("tib,tjb->tij", sketch_own, sketch_own, precision=highest)
    gram_copies = jnp.broadcast_to(gram_part[None], (wide_count,) + gram_part.shape)
    gram_matrix = lax.all_to_all(gram_copies, "wide", 0, 0, tiled=True).sum(axis=0)
    sketch_sum = wide_gather(sketch_own, wide_count)
    lower_factor = jnp.linalg.cholesky(gram_matrix)
    basis = jnp.einsum(
        "tij,tjb->tib", lower_inverse(lower_factor), sketch_sum, precision=highest
    )
    basis_round = basis.astype(jnp.bfloat16)
    own_basis = lax.dynamic_slice_in_dim(basis, lax.axis_index("wide") * share_cols, share_cols, 2)
    selected = jnp.einsum(
        "et,tkb->ekb",
        pick_target.astype(jnp.bfloat16),
        basis_round,
        preferred_element_type=jnp.float32,
    )
    selected = selected.astype(jnp.bfloat16)
    back_terms = jnp.einsum("eib,ekb->eik", factors, selected, preferred_element_type=jnp.float32)
    summed = jnp.einsum("ep,eik->pik", pair_pick, back_terms, precision=highest)
    summed = summed.reshape(panel_count, target_count, rank_dim, rank_dim)
    middle_terms = jnp.einsum("dtik,dij->dtkj", summed, coupling, precision=highest)
    partial_rows = jnp.einsum(
        "dtkj,djb->tkb", middle_terms, gathered.astype(jnp.float32), precision=highest
    )
    coeff_part = wide_reduce(partial_rows, wide_count)
    root_width = math.sqrt(full_width)
    return (own_basis * root_width, coeff_part / root_width)


def eliminate(gram):
    size = gram.shape[0]
    lane = lax.broadcasted_iota(jnp.int32, (size, size), 1)
    line = lax.broadcasted_iota(jnp.int32, (size, size), 0)
    eye = jnp.where(lane == line, 1.0, 0.0).astype(jnp.float32)
    whole = jnp.concatenate([gram, eye], axis=1)
    groups = [whole[8 * r : 8 * r + 8] for r in range(size // 8)]
    sub = lax.broadcasted_iota(jnp.int32, (8, 1), 0)
    for j in range(size):
        top, at = j // 8, j % 8
        row = groups[top][at : at + 1]
        scaled = row * (1.0 / row[:, j : j + 1])
        for r in range(top, size // 8):
            if r == top and at == 7:
                continue
            factor = groups[r][:, j : j + 1]
            if r == top:
                factor = jnp.where(sub > at, factor, 0.0)
            groups[r] = groups[r] - factor * scaled
    whole = jnp.concatenate(groups, axis=0)
    pivots = jnp.sum(jnp.where(lane == line, whole[:, :size], 0.0), axis=1, keepdims=True)
    return whole[:, size:] * (1.0 / jnp.sqrt(pivots))


def entry_order(panel, target, count, panels):
    slots = panel.shape[1]
    shape = (slots, slots)
    lane = lax.broadcasted_iota(jnp.int32, shape, 1)
    line = lax.broadcasted_iota(jnp.int32, shape, 0)
    across = jnp.where(lane[:1] < count, target * panels + panel, slots * panels)
    key = jnp.sum(jnp.where(line == lane, across, 0), axis=1, keepdims=True)
    ahead = (across < key) | ((across == key) & (lane < line))
    place = jnp.sum(ahead.astype(jnp.int32), axis=1, keepdims=True)
    order = jnp.sum(jnp.where(place == lane, line, 0), axis=0, keepdims=True)
    here = jnp.sum(jnp.where(place == lane, key + 1, 0), axis=0, keepdims=True)
    before = jnp.sum(jnp.where(place + 1 == lane, key + 1, 0), axis=0, keepdims=True)
    keep = (here == before).astype(jnp.int32)
    upto = jnp.sum((key <= lane).astype(jnp.int32), axis=0, keepdims=True)
    some = jnp.sum((key == lane).astype(jnp.int32), axis=0, keepdims=True)
    last = jnp.where(some > 0, upto - 1, slots)
    return order, keep, last


def recompress(
    f_hbm, panel_hbm, target_hbm, count_hbm, s_hbm, c_hbm, p_hbm, left, right,
    panel, target, count, order_vec, meta, coup, cbd, fbuf, cum, pbuf, sfull, scol, coef, ysend, yrecv, zsend, zrecv, total, qall, midall,
    loc_sem, small_sem, s_send, s_recv, c_send, c_recv, g_send, g_recv, y_sem, yr_sem, z_sem, zr_sem,
    q_send, q_recv, m_send, m_recv,
):
    slots = f_hbm.shape[0]
    rank = f_hbm.shape[2]
    width = f_hbm.shape[3]
    quarter = width // NARROW
    share = width // WAYS
    w = lax.axis_index("wide")
    n = lax.axis_index("narrow")
    z, y = w // YWAY, w % YWAY
    flip = w + 1 - 2 * y

    def zflip(m):
        return (z, z + 1 - 2 * (z % 2), (z + 2) % 4, 3 - z)[m]

    def remote(src, dst, send, recv, wide_at, narrow_at):
        return pltpu.make_async_remote_copy(
            src_ref=src, dst_ref=dst, send_sem=send, recv_sem=recv,
            device_id=(wide_at, narrow_at), device_id_type=pl.DeviceIdType.MESH,
        )

    barrier = pltpu.get_barrier_semaphore()
    for k in range(1, NARROW):
        pl.semaphore_signal(
            barrier, inc=1, device_id=(w, (n + k) % NARROW), device_id_type=pl.DeviceIdType.MESH
        )
    for k in range(1, WAYS):
        pl.semaphore_signal(
            barrier, inc=1, device_id=((w + k) % WAYS, n), device_id_type=pl.DeviceIdType.MESH
        )

    smalls = [
        pltpu.make_async_copy(src, dst, small_sem.at[i])
        for i, (src, dst) in enumerate(
            ((panel_hbm, panel), (target_hbm, target), (count_hbm, count), (c_hbm, coup))
        )
    ]
    step = slots // FSPLIT
    loads = [
        pltpu.make_async_copy(
            f_hbm.at[pl.ds(i * step, step)], fbuf.at[pl.ds(i * step, step)], loc_sem.at[i]
        )
        for i in range(FSPLIT)
    ]
    own_s = pltpu.make_async_copy(s_hbm, sfull.at[n], loc_sem.at[FSPLIT])
    load_p = pltpu.make_async_copy(p_hbm, pbuf, loc_sem.at[FSPLIT + 1])
    for c in smalls:
        c.start()
    own_s.start()
    for c in loads:
        c.start()
    load_p.start()

    pl.semaphore_wait(barrier, NARROW + WAYS - 2)

    twin, across = n + 1 - 2 * (n % 2), (n + 2) % NARROW
    twin_across = (twin + 2) % NARROW
    sent = []

    def s_send_to(src, ref, sem, to):
        c = remote(src, ref, s_send.at[sem], s_recv.at[sem], w, to)
        c.start()
        sent.append(c)

    def s_wait(ref, sem):
        remote(ref, ref, s_send.at[sem], s_recv.at[sem], w, twin).wait_recv()

    for p in range(coup.shape[0]):
        s_send_to(s_hbm.at[p], sfull.at[n, p], 3 * p, across)
        s_send_to(s_hbm.at[p], sfull.at[n, p], 3 * p + 1, twin)
    for c in smalls:
        c.wait()
    order_vec[...] = jnp.zeros(order_vec.shape, jnp.int32)
    for i, row in enumerate(entry_order(panel[...], target[...], count[...], coup.shape[0])):
        order_vec[i : i + 1, :slots] = row
    meta_copy = pltpu.make_async_copy(order_vec, meta, small_sem.at[4])
    meta_copy.start()
    empty = jnp.zeros((rank, rank), jnp.float32)
    cbd[:rank] = jnp.concatenate([coup[0], empty], axis=1)
    cbd[rank:] = jnp.concatenate([empty, coup[1]], axis=1)
    cum[slots] = jnp.zeros((2, rank, width), jnp.bfloat16)
    meta_copy.wait()
    for c in loads:
        c.wait()
    for c0 in range(0, rank, 16):

        def add(s, acc):
            x = fbuf[meta[0, s], 0, pl.ds(c0, 16), :].astype(jnp.float32)
            acc = acc * meta[1, s].astype(jnp.float32) + x
            high = acc.astype(jnp.bfloat16)
            cum[s, 0, pl.ds(c0, 16), :] = high
            cum[s, 1, pl.ds(c0, 16), :] = (acc - high.astype(jnp.float32)).astype(jnp.bfloat16)
            return acc

        lax.fori_loop(0, slots, add, jnp.zeros((16, width), jnp.float32), unroll=2)

    def pair_rows(t):
        first, second = meta[2, 2 * t], meta[2, 2 * t + 1]
        return jnp.concatenate(
            [cum[first, 0], cum[second, 0], cum[first, 1], cum[second, 1]], axis=0
        )

    for p in range(coup.shape[0]):
        s_wait(sfull.at[across, p], 3 * p)
        s_send_to(sfull.at[across, p], sfull.at[across, p], 3 * p + 2, twin)
    load_p.wait()
    own_s.wait()

    def project(at):
        cols = pl.ds(pl.multiple_of(at * quarter, quarter), quarter)
        probe = pbuf[:, :, cols].reshape(-1, quarter)
        return lax.dot_general(
            probe, sfull[at].reshape(-1, quarter), LAST_DIMS, preferred_element_type=jnp.float32
        )

    projected = project(n)
    projected = projected + project(across)
    for at, sem in ((twin, 1), (twin_across, 2)):
        for p in range(coup.shape[0]):
            s_wait(sfull.at[at, p], 3 * p + sem)
        projected = projected + project(at)
    coef[...] = lax.dot_general(
        projected, cbd[...], LAST_DIMS, precision=HIGHEST, preferred_element_type=jnp.float32
    ).astype(jnp.bfloat16)

    def partial_sketch(t):
        lhs = coef[pl.ds(pl.multiple_of(t * rank, rank), rank), :]
        lhs = jnp.concatenate([lhs, lhs], axis=1)
        return jnp.dot(lhs, pair_rows(t), preferred_element_type=jnp.float32)

    order = (2, 3, 1, 0)
    cut = rank // RCUT
    y_copies, z_copies = {}, {}

    def y_stage(k):
        ysend[k] = partial_sketch(zflip(order[k]) * YWAY + (1 - y)).astype(jnp.bfloat16)
        for h in range(RCUT):
            at = pl.ds(h * cut, cut)
            c = remote(
                ysend.at[k, at], yrecv.at[k, at], y_sem.at[k, h], yr_sem.at[k, h], flip, n
            )
            c.start()
            sent.append(c)
            y_copies[k, h] = c

    def z_stage(k):
        to = zflip(order[k]) * YWAY + y
        own = partial_sketch(to)
        for h in range(RCUT):
            at = pl.ds(h * cut, cut)
            y_copies[k, h].wait_recv()
            summed = own[h * cut : (h + 1) * cut] + yrecv[k, at].astype(jnp.float32)
            if order[k]:
                zsend[k, at] = summed.astype(jnp.bfloat16)
                c = remote(
                    zsend.at[k, at], zrecv.at[k, at], z_sem.at[k, h], zr_sem.at[k, h], to, n
                )
                c.start()
                sent.append(c)
                z_copies[k, h] = c
            else:
                total[at] = summed

    y_stage(0)
    y_stage(1)
    for k in range(ZWAY):
        if k + 2 < ZWAY:
            y_stage(k + 2)
        z_stage(k)
    for k in (2, 0, 1):
        for h in range(RCUT):
            at = pl.ds(h * cut, cut)
            z_copies[k, h].wait_recv()
            total[at] += zrecv[k, at].astype(jnp.float32)

    part = rank // 2

    def s_part(to):
        cols = pl.ds(pl.multiple_of((to % 2) * share, share), share)
        rows = pl.ds(pl.multiple_of((n % 2) * part, part), part)
        return sfull.at[to // 2, n // 2, rows, cols]

    for k in range(1, WAYS):
        to = (w + k) % WAYS
        c = remote(s_part(to), scol.at[n, w], c_send.at[k], c_recv.at[k], to, n)
        c.start()
        sent.append(c)
    scol[n, w] = s_part(w)[...]

    sketch = total[...]
    gram = lax.dot_general(
        sketch, sketch, LAST_DIMS, precision=HIGHEST, preferred_element_type=jnp.float32
    )
    inverse = eliminate(gram)
    qall[w] = jnp.dot(
        inverse, sketch, precision=HIGHEST, preferred_element_type=jnp.float32
    ).astype(jnp.bfloat16)

    def middle(t):
        terms = lax.dot_general(
            qall[t], pair_rows(t), LAST_DIMS, preferred_element_type=jnp.float32
        )
        terms = terms[:, : 2 * rank] + terms[:, 2 * rank :]
        rows = jnp.dot(terms, cbd[...], precision=HIGHEST, preferred_element_type=jnp.float32)
        midall[w, pl.ds(pl.multiple_of(t * rank, rank), rank), :] = rows.astype(jnp.bfloat16)

    def arrivals(at):
        return (at, at + 1 - 2 * (at % 2), 2 - at // 2, 3 - 3 * (at // 2))

    inner = z % 3 != 0
    later = []

    def start(c, holds=None):
        if holds is None:
            c.start()
        else:
            pl.when(holds)(c.start)
        later.append((c, holds))

    def spread(ref, send, recv):
        start(remote(ref, ref, send(1), recv(z), (z + 1) % 4 * YWAY + y, n), z < ZWAY - 1)
        start(remote(ref, ref, send(2), recv(z), (z + 3) % 4 * YWAY + y, n), z > 0)
        start(remote(ref, ref, send(0), recv(ZWAY + z), flip, n))

    def pass_on(ref, j, src_z, send, recv):
        remote(ref, ref, send(0), recv(src_z), w, n).wait_recv()
        to = (3 - z if j == 1 else (3 * z + 1) % 4) * YWAY + y
        start(remote(ref, ref, send(1 + 2 * j), recv(src_z), to, n), inner)
        start(remote(ref, ref, send(2 + 2 * j), recv(ZWAY + src_z), flip, n))

    def take(ref, src_z, send, recv):
        remote(ref, ref, send(0), recv(ZWAY + src_z), w, n).wait_recv()

    def q_sems(h):
        return (lambda k: q_send.at[h, k]), (lambda k: q_recv.at[h, k])

    def q_piece(at, h):
        return qall.at[at, pl.ds(h * (rank // QCUT), rank // QCUT), :]

    def mid_sems(i):
        return (lambda k: m_send.at[i, k]), (lambda k: m_recv.at[i, k])

    def mid_piece(src_z, src_y, i):
        first = arrivals(src_z)[i] * YWAY * rank
        rows = pl.ds(pl.multiple_of(first, YWAY * rank), YWAY * rank)
        return midall.at[src_z * YWAY + src_y, rows, :]

    for h in range(QCUT):
        spread(q_piece(w, h), *q_sems(h))
    middle(w)
    for k in range(1, WAYS):
        src = scol.at[n, (w + WAYS - k) % WAYS]
        remote(src, src, c_send.at[k], c_recv.at[k], w, twin).wait_recv()
    for k in range(1, NARROW):
        c = remote(
            scol.at[n], scol.at[n], g_send.at[k], g_recv.at[k], w, (n + k) % NARROW
        )
        c.start()
        sent.append(c)

    def far_half(j):
        src_z = arrivals(z)[j]
        far = src_z * YWAY + 1 - y
        for h in range(QCUT):
            take(q_piece(far, h), src_z, *q_sems(h))
        middle(far)
        spread(mid_piece(z, y, j), *mid_sems(j))

    def mid_pass(i, j):
        src_z = arrivals(z)[j]
        pass_on(mid_piece(src_z, y, i), j, src_z, *mid_sems(i))

    for j in range(1, ZWAY):
        src_z = arrivals(z)[j]
        near = src_z * YWAY + y
        for h in range(QCUT):
            pass_on(q_piece(near, h), j, src_z, *q_sems(h))
        far_half(j - 1)
        middle(near)
    for j in range(1, ZWAY):
        mid_pass(0, j)
    far_half(ZWAY - 1)
    for i in range(1, ZWAY):
        for j in range(1, ZWAY):
            mid_pass(i, j)

    for k in range(WAYS):
        cols = pl.ds(pl.multiple_of(w * share, share), share)
        left[k] = qall[k, :, cols]

    def rows_of(src):
        shared = jnp.concatenate([scol[k, src] for k in range(NARROW)], axis=0)
        return jnp.dot(midall[src], shared, preferred_element_type=jnp.float32)

    for k in range(1, NARROW):
        src = scol.at[(n + NARROW - k) % NARROW]
        remote(src, src, g_send.at[k], g_recv.at[k], w, twin).wait_recv()
    rows = rows_of(w)
    for j, src_z in enumerate(arrivals(z)):
        if j:
            rows = rows + rows_of(src_z * YWAY + y)
    for src_z in arrivals(z):
        for i in range(ZWAY):
            take(mid_piece(src_z, 1 - y, i), src_z, *mid_sems(i))
        rows = rows + rows_of(src_z * YWAY + 1 - y)
    right[...] = rows.reshape(right.shape)
    for c in sent:
        c.wait_send()
    for c, holds in later:
        if holds is None:
            c.wait_send()
        else:
            pl.when(holds)(c.wait_send)


def fused(entry_factor, entry_panel, entry_target, entry_count, panel_shared, coupling, probes):
    slots, _, rank, width = entry_factor.shape
    panels = panel_shared.shape[0]
    targets = probes.shape[0]
    share = width // WAYS
    depth = panels * rank
    bf16, f32, i32 = jnp.bfloat16, jnp.float32, jnp.int32
    dma = pltpu.SemaphoreType.DMA
    left, right = pl.pallas_call(
        recompress,
        out_shape=(
            jax.ShapeDtypeStruct((targets, rank, share), bf16),
            jax.ShapeDtypeStruct((targets, rank, share), f32),
        ),
        in_specs=[pl.BlockSpec(memory_space=pltpu.HBM)] * 7,
        out_specs=(
            pl.BlockSpec(memory_space=pltpu.VMEM),
            pl.BlockSpec(memory_space=pltpu.VMEM),
        ),
        scratch_shapes=[
            pltpu.VMEM((1, slots), i32),
            pltpu.VMEM((1, slots), i32),
            pltpu.VMEM((1, 1), i32),
            pltpu.VMEM((8, 128), i32),
            pltpu.SMEM((8, 128), i32),
            pltpu.VMEM((panels, rank, rank), f32),
            pltpu.VMEM((depth, depth), f32),
            pltpu.VMEM((slots, 1, rank, width), bf16),
            pltpu.VMEM((slots + 1, 2, rank, width), bf16),
            pltpu.VMEM((targets, rank, width), bf16),
            pltpu.VMEM((NARROW, panels, rank, width // NARROW), bf16),
            pltpu.VMEM((NARROW, WAYS, depth // NARROW, share), bf16),
            pltpu.VMEM((targets * rank, depth), bf16),
            pltpu.VMEM((ZWAY, rank, width), bf16),
            pltpu.VMEM((ZWAY, rank, width), bf16),
            pltpu.VMEM((ZWAY - 1, rank, width), bf16),
            pltpu.VMEM((ZWAY - 1, rank, width), bf16),
            pltpu.VMEM((rank, width), f32),
            pltpu.VMEM((targets, rank, width), bf16),
            pltpu.VMEM((WAYS, targets * rank, depth), bf16),
            dma((FSPLIT + 2,)),
            dma((5,)),
            dma((3 * panels,)),
            dma((3 * panels,)),
            dma((WAYS,)),
            dma((WAYS,)),
            dma((NARROW,)),
            dma((NARROW,)),
            dma((ZWAY, RCUT)),
            dma((ZWAY, RCUT)),
            dma((ZWAY, RCUT)),
            dma((ZWAY, RCUT)),
            dma((QCUT, 9)),
            dma((QCUT, WAYS)),
            dma((ZWAY, 9)),
            dma((ZWAY, WAYS)),
        ],
        compiler_params=pltpu.CompilerParams(
            collective_id=0, has_side_effects=True, vmem_limit_bytes=63 * 1024 * 1024
        ),
        name="recompress",
    )(entry_factor, entry_panel.T, entry_target.T, entry_count, panel_shared, coupling, probes)
    root_width = math.sqrt(width)
    return (left.astype(f32) * root_width, right / root_width)


def solution(mesh):
    placed = (
        P("wide", "narrow", None, None),
        P("wide", "narrow"),
        P("wide", "narrow"),
        P("narrow", "wide"),
        P("wide", None, "narrow"),
        P("wide", None, None),
        P("narrow", None, None),
    )
    return jax.shard_map(
        fused if mesh.shape["wide"] == WAYS and mesh.shape["narrow"] == NARROW else shards,
        mesh=mesh,
        in_specs=placed,
        out_specs=(P("narrow", None, "wide"), P("narrow", None, "wide")),
        check_vma=False,
    )
```

```python
import functools
import math

import jax
import jax.numpy as jnp
from jax import lax
from jax.experimental import pallas as pl
from jax.experimental.pallas import tpu as pltpu
from jax.sharding import PartitionSpec as P

HIGHEST = lax.Precision.HIGHEST
LAST_DIMS = (((1,), (1,)), ((), ()))
ZWAY = 4
YWAY = 2
WAYS = ZWAY * YWAY
NARROW = 4
FSPLIT = 4
RCUT = 2
QCUT = 2

def wide_reduce(x, count):
    lead, rows, width = x.shape
    pieces = x.reshape(lead, rows, count, width // count).transpose(2, 0, 1, 3)
    pieces = lax.all_to_all(pieces, "wide", 0, 0, tiled=True)
    return pieces.sum(axis=0)


def wide_gather(x, count):
    lead, rows, width = x.shape
    copies = jnp.broadcast_to(x[None], (count, lead, rows, width))
    copies = lax.all_to_all(copies, "wide", 0, 0, tiled=True)
    return copies.transpose(1, 2, 0, 3).reshape(lead, rows, count * width)


def lower_inverse(lower):
    highest = lax.Precision.HIGHEST
    size = lower.shape[-1]
    eye = jnp.eye(size, dtype=lower.dtype)
    diag = jnp.diagonal(lower, axis1=-2, axis2=-1)
    strict = eye - lower / diag[..., :, None]
    unit_inverse = eye + strict
    power = strict
    for _ in range(max(size - 1, 1).bit_length() - 1):
        power = jnp.einsum("tij,tjk->tik", power, power, precision=highest)
        unit_inverse = unit_inverse + jnp.einsum(
            "tij,tjk->tik", unit_inverse, power, precision=highest
        )
    return unit_inverse / diag[..., None, :]


def shards(entry_factor, entry_panel, entry_target, entry_count, panel_shared, coupling, probes):
    highest = lax.Precision.HIGHEST
    factors = entry_factor[:, 0]
    slot_count = factors.shape[0]
    rank_dim = factors.shape[1]
    full_width = factors.shape[2]
    panel_count = panel_shared.shape[0]
    target_count = probes.shape[0]
    live_mask = (jnp.arange(slot_count) < entry_count[0, 0]).astype(jnp.float32)
    pick_panel = (entry_panel == jnp.arange(panel_count)[None, :]).astype(jnp.float32) * live_mask[
        :, None
    ]
    pick_target = (entry_target == jnp.arange(target_count)[None, :]).astype(jnp.float32)
    pair_pick = (pick_panel[:, :, None] * pick_target[:, None, :]).reshape(
        slot_count, panel_count * target_count
    )
    gathered = lax.all_gather(panel_shared, "narrow", axis=2, tiled=True)
    projected = jnp.einsum("drb,tkb->dtrk", gathered, probes, preferred_element_type=jnp.float32)
    coefficients = jnp.einsum("dij,dtjk->dtik", coupling, projected, precision=highest).astype(
        jnp.bfloat16
    )
    coeff_table = coefficients.reshape(panel_count * target_count, rank_dim * rank_dim)
    chosen = jnp.dot(
        pair_pick.astype(jnp.bfloat16), coeff_table, preferred_element_type=jnp.float32
    )
    chosen = chosen.astype(jnp.bfloat16).reshape(slot_count, rank_dim, rank_dim)
    contributions = jnp.einsum("eji,ejb->eib", chosen, factors, preferred_element_type=jnp.float32)
    sketch = jnp.einsum("et,eib->tib", pick_target, contributions, precision=highest)
    wide_count = lax.axis_size("wide")
    share_cols = full_width // wide_count
    sketch_own = wide_reduce(sketch, wide_count)
    gram_part = jnp.einsum("tib,tjb->tij", sketch_own, sketch_own, precision=highest)
    gram_copies = jnp.broadcast_to(gram_part[None], (wide_count,) + gram_part.shape)
    gram_matrix = lax.all_to_all(gram_copies, "wide", 0, 0, tiled=True).sum(axis=0)
    sketch_sum = wide_gather(sketch_own, wide_count)
    lower_factor = jnp.linalg.cholesky(gram_matrix)
    basis = jnp.einsum(
        "tij,tjb->tib", lower_inverse(lower_factor), sketch_sum, precision=highest
    )
    basis_round = basis.astype(jnp.bfloat16)
    own_basis = lax.dynamic_slice_in_dim(basis, lax.axis_index("wide") * share_cols, share_cols, 2)
    selected = jnp.einsum(
        "et,tkb->ekb",
        pick_target.astype(jnp.bfloat16),
        basis_round,
        preferred_element_type=jnp.float32,
    )
    selected = selected.astype(jnp.bfloat16)
    back_terms = jnp.einsum("eib,ekb->eik", factors, selected, preferred_element_type=jnp.float32)
    summed = jnp.einsum("ep,eik->pik", pair_pick, back_terms, precision=highest)
    summed = summed.reshape(panel_count, target_count, rank_dim, rank_dim)
    middle_terms = jnp.einsum("dtik,dij->dtkj", summed, coupling, precision=highest)
    partial_rows = jnp.einsum(
        "dtkj,djb->tkb", middle_terms, gathered.astype(jnp.float32), precision=highest
    )
    coeff_part = wide_reduce(partial_rows, wide_count)
    root_width = math.sqrt(full_width)
    return (own_basis * root_width, coeff_part / root_width)


def eliminate(gram):
    size = gram.shape[0]
    step = 8
    lane = lax.broadcasted_iota(jnp.int32, (size, size), 1)
    line = lax.broadcasted_iota(jnp.int32, (size, size), 0)
    eye = jnp.where(lane == line, 1.0, 0.0).astype(jnp.float32)
    whole = jnp.concatenate([gram, eye], axis=1)
    groups = [whole[r : r + step] for r in range(0, size, step)]
    for top, group in enumerate(groups):
        first = top * step
        rows = [group[p : p + 1] for p in range(step)]
        block = [
            [jnp.broadcast_to(row[:, first + q : first + q + 1], row.shape) for q in range(step)]
            for row in rows
        ]
        inverse = []
        ratio = {}
        for p in range(step):
            inverse.append(1.0 / block[p][p])
            for q in range(p + 1, step):
                ratio[p, q] = block[p][q] * inverse[p]
                rows[q] = rows[q] - ratio[p, q] * rows[p]
                for s in range(q, step):
                    block[q][s] = block[q][s] - ratio[p, q] * block[p][s]
        solved = [None] * step
        for p in reversed(range(step)):
            solved[p] = rows[p] * inverse[p]
            for q in range(p + 1, step):
                solved[p] = solved[p] - ratio[p, q] * solved[q]
        groups[top] = jnp.concatenate(rows, axis=0)
        for r in range(top + 1, size // step):
            change = groups[r][:, first : first + 1] * solved[0]
            for p in range(1, step):
                change = change + groups[r][:, first + p : first + p + 1] * solved[p]
            groups[r] = groups[r] - change
    whole = jnp.concatenate(groups, axis=0)
    pivots = jnp.sum(jnp.where(lane == line, whole[:, :size], 0.0), axis=1, keepdims=True)
    return whole[:, size:] * (1.0 / jnp.sqrt(pivots))


def entry_order(panel, target, count, panels):
    slots = panel.shape[1]
    shape = (slots, slots)
    lane = lax.broadcasted_iota(jnp.int32, shape, 1)
    line = lax.broadcasted_iota(jnp.int32, shape, 0)
    across = jnp.where(lane[:1] < count, target * panels + panel, slots * panels)
    key = jnp.sum(jnp.where(line == lane, across, 0), axis=1, keepdims=True)
    ahead = (across < key) | ((across == key) & (lane < line))
    place = jnp.sum(ahead.astype(jnp.int32), axis=1, keepdims=True)
    order = jnp.sum(jnp.where(place == lane, line, 0), axis=0, keepdims=True)
    here = jnp.sum(jnp.where(place == lane, key + 1, 0), axis=0, keepdims=True)
    before = jnp.sum(jnp.where(place + 1 == lane, key + 1, 0), axis=0, keepdims=True)
    keep = (here == before).astype(jnp.int32)
    upto = jnp.sum((key <= lane).astype(jnp.int32), axis=0, keepdims=True)
    some = jnp.sum((key == lane).astype(jnp.int32), axis=0, keepdims=True)
    last = jnp.where(some > 0, upto - 1, slots)
    return order, keep, last


def recompress(
    f_hbm, panel_hbm, target_hbm, count_hbm, s_hbm, c_hbm, p_hbm, left, right,
    panel, target, count, order_vec, meta, coup, cbd, fbuf, cum, pbuf, sfull, scol, coef, ysend, yrecv, zsend, zrecv, total, qall, midall,
    loc_sem, small_sem, s_send, s_recv, c_send, c_recv, g_send, g_recv, y_sem, yr_sem, z_sem, zr_sem,
    q_send, q_recv, m_send, m_recv,
):
    slots = f_hbm.shape[0]
    rank = f_hbm.shape[2]
    width = f_hbm.shape[3]
    quarter = width // NARROW
    share = width // WAYS
    w = lax.axis_index("wide")
    n = lax.axis_index("narrow")
    z, y = w // YWAY, w % YWAY
    flip = w + 1 - 2 * y

    def zflip(m):
        return (z, z + 1 - 2 * (z % 2), (z + 2) % 4, 3 - z)[m]

    def remote(src, dst, send, recv, wide_at, narrow_at):
        return pltpu.make_async_remote_copy(
            src_ref=src, dst_ref=dst, send_sem=send, recv_sem=recv,
            device_id=(wide_at, narrow_at), device_id_type=pl.DeviceIdType.MESH,
        )

    barrier = pltpu.get_barrier_semaphore()
    for k in range(1, NARROW):
        pl.semaphore_signal(
            barrier, inc=1, device_id=(w, (n + k) % NARROW), device_id_type=pl.DeviceIdType.MESH
        )
    for k in range(1, WAYS):
        pl.semaphore_signal(
            barrier, inc=1, device_id=((w + k) % WAYS, n), device_id_type=pl.DeviceIdType.MESH
        )

    smalls = [
        pltpu.make_async_copy(src, dst, small_sem.at[i])
        for i, (src, dst) in enumerate(
            ((panel_hbm, panel), (target_hbm, target), (count_hbm, count), (c_hbm, coup))
        )
    ]
    step = slots // FSPLIT
    loads = [
        pltpu.make_async_copy(
            f_hbm.at[pl.ds(i * step, step)], fbuf.at[pl.ds(i * step, step)], loc_sem.at[i]
        )
        for i in range(FSPLIT)
    ]
    own_s = pltpu.make_async_copy(s_hbm, sfull.at[n], loc_sem.at[FSPLIT])
    load_p = pltpu.make_async_copy(p_hbm, pbuf, loc_sem.at[FSPLIT + 1])
    for c in smalls:
        c.start()
    own_s.start()
    for c in loads:
        c.start()
    load_p.start()

    pl.semaphore_wait(barrier, NARROW + WAYS - 2)

    twin, across = n + 1 - 2 * (n % 2), (n + 2) % NARROW
    twin_across = (twin + 2) % NARROW
    sent = []

    def s_send_to(src, ref, sem, to):
        c = remote(src, ref, s_send.at[sem], s_recv.at[sem], w, to)
        c.start()
        sent.append(c)

    def s_wait(ref, sem):
        remote(ref, ref, s_send.at[sem], s_recv.at[sem], w, twin).wait_recv()

    for p in range(coup.shape[0]):
        s_send_to(s_hbm.at[p], sfull.at[n, p], 3 * p, across)
        s_send_to(s_hbm.at[p], sfull.at[n, p], 3 * p + 1, twin)
    for c in smalls:
        c.wait()
    order_vec[...] = jnp.zeros(order_vec.shape, jnp.int32)
    for i, row in enumerate(entry_order(panel[...], target[...], count[...], coup.shape[0])):
        order_vec[i : i + 1, :slots] = row
    meta_copy = pltpu.make_async_copy(order_vec, meta, small_sem.at[4])
    meta_copy.start()
    empty = jnp.zeros((rank, rank), jnp.float32)
    cbd[:rank] = jnp.concatenate([coup[0], empty], axis=1)
    cbd[rank:] = jnp.concatenate([empty, coup[1]], axis=1)
    cum[slots] = jnp.zeros((2, rank, width), jnp.bfloat16)
    meta_copy.wait()
    for c in loads:
        c.wait()
    for c0 in range(0, rank, 16):

        def add(s, acc):
            x = fbuf[meta[0, s], 0, pl.ds(c0, 16), :].astype(jnp.float32)
            acc = acc * meta[1, s].astype(jnp.float32) + x
            high = acc.astype(jnp.bfloat16)
            cum[s, 0, pl.ds(c0, 16), :] = high
            cum[s, 1, pl.ds(c0, 16), :] = (acc - high.astype(jnp.float32)).astype(jnp.bfloat16)
            return acc

        lax.fori_loop(0, slots, add, jnp.zeros((16, width), jnp.float32), unroll=2)

    def pair_rows(t):
        first, second = meta[2, 2 * t], meta[2, 2 * t + 1]
        return jnp.concatenate(
            [cum[first, 0], cum[second, 0], cum[first, 1], cum[second, 1]], axis=0
        )

    for p in range(coup.shape[0]):
        s_wait(sfull.at[across, p], 3 * p)
        s_send_to(sfull.at[across, p], sfull.at[across, p], 3 * p + 2, twin)
    load_p.wait()
    own_s.wait()

    def project(at):
        cols = pl.ds(pl.multiple_of(at * quarter, quarter), quarter)
        probe = pbuf[:, :, cols].reshape(-1, quarter)
        return lax.dot_general(
            probe, sfull[at].reshape(-1, quarter), LAST_DIMS, preferred_element_type=jnp.float32
        )

    projected = project(n)
    projected = projected + project(across)
    for at, sem in ((twin, 1), (twin_across, 2)):
        for p in range(coup.shape[0]):
            s_wait(sfull.at[at, p], 3 * p + sem)
        projected = projected + project(at)
    coef[...] = lax.dot_general(
        projected, cbd[...], LAST_DIMS, precision=HIGHEST, preferred_element_type=jnp.float32
    ).astype(jnp.bfloat16)

    def partial_sketch(t):
        lhs = coef[pl.ds(pl.multiple_of(t * rank, rank), rank), :]
        lhs = jnp.concatenate([lhs, lhs], axis=1)
        return jnp.dot(lhs, pair_rows(t), preferred_element_type=jnp.float32)

    order = (2, 3, 1, 0)
    cut = rank // RCUT
    y_copies, z_copies = {}, {}

    def y_stage(k):
        ysend[k] = partial_sketch(zflip(order[k]) * YWAY + (1 - y)).astype(jnp.bfloat16)
        for h in range(RCUT):
            at = pl.ds(h * cut, cut)
            c = remote(
                ysend.at[k, at], yrecv.at[k, at], y_sem.at[k, h], yr_sem.at[k, h], flip, n
            )
            c.start()
            sent.append(c)
            y_copies[k, h] = c

    def z_stage(k):
        to = zflip(order[k]) * YWAY + y
        own = partial_sketch(to)
        for h in range(RCUT):
            at = pl.ds(h * cut, cut)
            y_copies[k, h].wait_recv()
            summed = own[h * cut : (h + 1) * cut] + yrecv[k, at].astype(jnp.float32)
            if order[k]:
                zsend[k, at] = summed.astype(jnp.bfloat16)
                c = remote(
                    zsend.at[k, at], zrecv.at[k, at], z_sem.at[k, h], zr_sem.at[k, h], to, n
                )
                c.start()
                sent.append(c)
                z_copies[k, h] = c
            else:
                total[at] = summed

    y_stage(0)
    y_stage(1)
    for k in range(ZWAY):
        if k + 2 < ZWAY:
            y_stage(k + 2)
        z_stage(k)
    for k in (2, 0, 1):
        for h in range(RCUT):
            at = pl.ds(h * cut, cut)
            z_copies[k, h].wait_recv()
            total[at] += zrecv[k, at].astype(jnp.float32)

    part = rank // 2

    def s_part(to):
        cols = pl.ds(pl.multiple_of((to % 2) * share, share), share)
        rows = pl.ds(pl.multiple_of((n % 2) * part, part), part)
        return sfull.at[to // 2, n // 2, rows, cols]

    for k in range(1, WAYS):
        to = (w + k) % WAYS
        c = remote(s_part(to), scol.at[n, w], c_send.at[k], c_recv.at[k], to, n)
        c.start()
        sent.append(c)
    scol[n, w] = s_part(w)[...]

    sketch = total[...]
    gram = lax.dot_general(
        sketch, sketch, LAST_DIMS, precision=HIGHEST, preferred_element_type=jnp.float32
    )
    inverse = eliminate(gram)
    qall[w] = jnp.dot(
        inverse, sketch, precision=HIGHEST, preferred_element_type=jnp.float32
    ).astype(jnp.bfloat16)

    def middle(t):
        terms = lax.dot_general(
            qall[t], pair_rows(t), LAST_DIMS, preferred_element_type=jnp.float32
        )
        terms = terms[:, : 2 * rank] + terms[:, 2 * rank :]
        rows = jnp.dot(terms, cbd[...], precision=HIGHEST, preferred_element_type=jnp.float32)
        midall[w, pl.ds(pl.multiple_of(t * rank, rank), rank), :] = rows.astype(jnp.bfloat16)

    def arrivals(at):
        return (at, at + 1 - 2 * (at % 2), 2 - at // 2, 3 - 3 * (at // 2))

    inner = z % 3 != 0
    later = []

    def start(c, holds=None):
        if holds is None:
            c.start()
        else:
            pl.when(holds)(c.start)
        later.append((c, holds))

    def spread(ref, send, recv):
        start(remote(ref, ref, send(1), recv(z), (z + 1) % 4 * YWAY + y, n), z < ZWAY - 1)
        start(remote(ref, ref, send(2), recv(z), (z + 3) % 4 * YWAY + y, n), z > 0)
        start(remote(ref, ref, send(0), recv(ZWAY + z), flip, n))

    def pass_on(ref, j, src_z, send, recv):
        remote(ref, ref, send(0), recv(src_z), w, n).wait_recv()
        to = (3 - z if j == 1 else (3 * z + 1) % 4) * YWAY + y
        start(remote(ref, ref, send(1 + 2 * j), recv(src_z), to, n), inner)
        start(remote(ref, ref, send(2 + 2 * j), recv(ZWAY + src_z), flip, n))

    def take(ref, src_z, send, recv):
        remote(ref, ref, send(0), recv(ZWAY + src_z), w, n).wait_recv()

    def q_sems(h):
        return (lambda k: q_send.at[h, k]), (lambda k: q_recv.at[h, k])

    def q_piece(at, h):
        return qall.at[at, pl.ds(h * (rank // QCUT), rank // QCUT), :]

    def mid_sems(i):
        return (lambda k: m_send.at[i, k]), (lambda k: m_recv.at[i, k])

    def mid_piece(src_z, src_y, i):
        first = arrivals(src_z)[i] * YWAY * rank
        rows = pl.ds(pl.multiple_of(first, YWAY * rank), YWAY * rank)
        return midall.at[src_z * YWAY + src_y, rows, :]

    for h in range(QCUT):
        spread(q_piece(w, h), *q_sems(h))
    middle(w)
    for k in range(1, WAYS):
        src = scol.at[n, (w + WAYS - k) % WAYS]
        remote(src, src, c_send.at[k], c_recv.at[k], w, twin).wait_recv()
    for k in range(1, NARROW):
        c = remote(
            scol.at[n], scol.at[n], g_send.at[k], g_recv.at[k], w, (n + k) % NARROW
        )
        c.start()
        sent.append(c)

    def far_half(j):
        src_z = arrivals(z)[j]
        far = src_z * YWAY + 1 - y
        for h in range(QCUT):
            take(q_piece(far, h), src_z, *q_sems(h))
        middle(far)
        spread(mid_piece(z, y, j), *mid_sems(j))

    def mid_pass(i, j):
        src_z = arrivals(z)[j]
        pass_on(mid_piece(src_z, y, i), j, src_z, *mid_sems(i))

    for j in range(1, ZWAY):
        src_z = arrivals(z)[j]
        near = src_z * YWAY + y
        for h in range(QCUT):
            pass_on(q_piece(near, h), j, src_z, *q_sems(h))
        far_half(j - 1)
        middle(near)
    for j in range(1, ZWAY):
        mid_pass(0, j)
    far_half(ZWAY - 1)
    for i in range(1, ZWAY):
        for j in range(1, ZWAY):
            mid_pass(i, j)

    for k in range(WAYS):
        cols = pl.ds(pl.multiple_of(w * share, share), share)
        left[k] = qall[k, :, cols]

    def rows_of(src):
        shared = jnp.concatenate([scol[k, src] for k in range(NARROW)], axis=0)
        return jnp.dot(midall[src], shared, preferred_element_type=jnp.float32)

    for k in range(1, NARROW):
        src = scol.at[(n + NARROW - k) % NARROW]
        remote(src, src, g_send.at[k], g_recv.at[k], w, twin).wait_recv()
    rows = rows_of(w)
    for j, src_z in enumerate(arrivals(z)):
        if j:
            rows = rows + rows_of(src_z * YWAY + y)
    for src_z in arrivals(z):
        for i in range(ZWAY):
            take(mid_piece(src_z, 1 - y, i), src_z, *mid_sems(i))
        rows = rows + rows_of(src_z * YWAY + 1 - y)
    right[...] = rows.reshape(right.shape)
    for c in sent:
        c.wait_send()
    for c, holds in later:
        if holds is None:
            c.wait_send()
        else:
            pl.when(holds)(c.wait_send)


def fused(entry_factor, entry_panel, entry_target, entry_count, panel_shared, coupling, probes):
    slots, _, rank, width = entry_factor.shape
    panels = panel_shared.shape[0]
    targets = probes.shape[0]
    share = width // WAYS
    depth = panels * rank
    bf16, f32, i32 = jnp.bfloat16, jnp.float32, jnp.int32
    dma = pltpu.SemaphoreType.DMA
    left, right = pl.pallas_call(
        recompress,
        out_shape=(
            jax.ShapeDtypeStruct((targets, rank, share), bf16),
            jax.ShapeDtypeStruct((targets, rank, share), f32),
        ),
        in_specs=[pl.BlockSpec(memory_space=pltpu.HBM)] * 7,
        out_specs=(
            pl.BlockSpec(memory_space=pltpu.VMEM),
            pl.BlockSpec(memory_space=pltpu.VMEM),
        ),
        scratch_shapes=[
            pltpu.VMEM((1, slots), i32),
            pltpu.VMEM((1, slots), i32),
            pltpu.VMEM((1, 1), i32),
            pltpu.VMEM((8, 128), i32),
            pltpu.SMEM((8, 128), i32),
            pltpu.VMEM((panels, rank, rank), f32),
            pltpu.VMEM((depth, depth), f32),
            pltpu.VMEM((slots, 1, rank, width), bf16),
            pltpu.VMEM((slots + 1, 2, rank, width), bf16),
            pltpu.VMEM((targets, rank, width), bf16),
            pltpu.VMEM((NARROW, panels, rank, width // NARROW), bf16),
            pltpu.VMEM((NARROW, WAYS, depth // NARROW, share), bf16),
            pltpu.VMEM((targets * rank, depth), bf16),
            pltpu.VMEM((ZWAY, rank, width), bf16),
            pltpu.VMEM((ZWAY, rank, width), bf16),
            pltpu.VMEM((ZWAY - 1, rank, width), bf16),
            pltpu.VMEM((ZWAY - 1, rank, width), bf16),
            pltpu.VMEM((rank, width), f32),
            pltpu.VMEM((targets, rank, width), bf16),
            pltpu.VMEM((WAYS, targets * rank, depth), bf16),
            dma((FSPLIT + 2,)),
            dma((5,)),
            dma((3 * panels,)),
            dma((3 * panels,)),
            dma((WAYS,)),
            dma((WAYS,)),
            dma((NARROW,)),
            dma((NARROW,)),
            dma((ZWAY, RCUT)),
            dma((ZWAY, RCUT)),
            dma((ZWAY, RCUT)),
            dma((ZWAY, RCUT)),
            dma((QCUT, 9)),
            dma((QCUT, WAYS)),
            dma((ZWAY, 9)),
            dma((ZWAY, WAYS)),
        ],
        compiler_params=pltpu.CompilerParams(
            collective_id=0, has_side_effects=True, vmem_limit_bytes=63 * 1024 * 1024
        ),
        name="recompress",
    )(entry_factor, entry_panel.T, entry_target.T, entry_count, panel_shared, coupling, probes)
    root_width = math.sqrt(width)
    return (left.astype(f32) * root_width, right / root_width)


def solution(mesh):
    placed = (
        P("wide", "narrow", None, None),
        P("wide", "narrow"),
        P("wide", "narrow"),
        P("narrow", "wide"),
        P("wide", None, "narrow"),
        P("wide", None, None),
        P("narrow", None, None),
    )
    return jax.shard_map(
        fused if mesh.shape["wide"] == WAYS and mesh.shape["narrow"] == NARROW else shards,
        mesh=mesh,
        in_specs=placed,
        out_specs=(P("narrow", None, "wide"), P("narrow", None, "wide")),
        check_vma=False,
    )
```

```python
import functools
import math

import jax
import jax.numpy as jnp
from jax import lax
from jax.experimental import pallas as pl
from jax.experimental.pallas import tpu as pltpu
from jax.sharding import PartitionSpec as P

HIGHEST = lax.Precision.HIGHEST
LAST_DIMS = (((1,), (1,)), ((), ()))
ZWAY = 4
YWAY = 2
WAYS = ZWAY * YWAY
NARROW = 4
FSPLIT = 4
RCUT = 2
QCUT = 4
ROUTES = "LDDD"

def wide_reduce(x, count):
    lead, rows, width = x.shape
    pieces = x.reshape(lead, rows, count, width // count).transpose(2, 0, 1, 3)
    pieces = lax.all_to_all(pieces, "wide", 0, 0, tiled=True)
    return pieces.sum(axis=0)


def wide_gather(x, count):
    lead, rows, width = x.shape
    copies = jnp.broadcast_to(x[None], (count, lead, rows, width))
    copies = lax.all_to_all(copies, "wide", 0, 0, tiled=True)
    return copies.transpose(1, 2, 0, 3).reshape(lead, rows, count * width)


def lower_inverse(lower):
    highest = lax.Precision.HIGHEST
    size = lower.shape[-1]
    eye = jnp.eye(size, dtype=lower.dtype)
    diag = jnp.diagonal(lower, axis1=-2, axis2=-1)
    strict = eye - lower / diag[..., :, None]
    unit_inverse = eye + strict
    power = strict
    for _ in range(max(size - 1, 1).bit_length() - 1):
        power = jnp.einsum("tij,tjk->tik", power, power, precision=highest)
        unit_inverse = unit_inverse + jnp.einsum(
            "tij,tjk->tik", unit_inverse, power, precision=highest
        )
    return unit_inverse / diag[..., None, :]


def shards(entry_factor, entry_panel, entry_target, entry_count, panel_shared, coupling, probes):
    highest = lax.Precision.HIGHEST
    factors = entry_factor[:, 0]
    slot_count = factors.shape[0]
    rank_dim = factors.shape[1]
    full_width = factors.shape[2]
    panel_count = panel_shared.shape[0]
    target_count = probes.shape[0]
    live_mask = (jnp.arange(slot_count) < entry_count[0, 0]).astype(jnp.float32)
    pick_panel = (entry_panel == jnp.arange(panel_count)[None, :]).astype(jnp.float32) * live_mask[
        :, None
    ]
    pick_target = (entry_target == jnp.arange(target_count)[None, :]).astype(jnp.float32)
    pair_pick = (pick_panel[:, :, None] * pick_target[:, None, :]).reshape(
        slot_count, panel_count * target_count
    )
    gathered = lax.all_gather(panel_shared, "narrow", axis=2, tiled=True)
    projected = jnp.einsum("drb,tkb->dtrk", gathered, probes, preferred_element_type=jnp.float32)
    coefficients = jnp.einsum("dij,dtjk->dtik", coupling, projected, precision=highest).astype(
        jnp.bfloat16
    )
    coeff_table = coefficients.reshape(panel_count * target_count, rank_dim * rank_dim)
    chosen = jnp.dot(
        pair_pick.astype(jnp.bfloat16), coeff_table, preferred_element_type=jnp.float32
    )
    chosen = chosen.astype(jnp.bfloat16).reshape(slot_count, rank_dim, rank_dim)
    contributions = jnp.einsum("eji,ejb->eib", chosen, factors, preferred_element_type=jnp.float32)
    sketch = jnp.einsum("et,eib->tib", pick_target, contributions, precision=highest)
    wide_count = lax.axis_size("wide")
    share_cols = full_width // wide_count
    sketch_own = wide_reduce(sketch, wide_count)
    gram_part = jnp.einsum("tib,tjb->tij", sketch_own, sketch_own, precision=highest)
    gram_copies = jnp.broadcast_to(gram_part[None], (wide_count,) + gram_part.shape)
    gram_matrix = lax.all_to_all(gram_copies, "wide", 0, 0, tiled=True).sum(axis=0)
    sketch_sum = wide_gather(sketch_own, wide_count)
    lower_factor = jnp.linalg.cholesky(gram_matrix)
    basis = jnp.einsum(
        "tij,tjb->tib", lower_inverse(lower_factor), sketch_sum, precision=highest
    )
    basis_round = basis.astype(jnp.bfloat16)
    own_basis = lax.dynamic_slice_in_dim(basis, lax.axis_index("wide") * share_cols, share_cols, 2)
    selected = jnp.einsum(
        "et,tkb->ekb",
        pick_target.astype(jnp.bfloat16),
        basis_round,
        preferred_element_type=jnp.float32,
    )
    selected = selected.astype(jnp.bfloat16)
    back_terms = jnp.einsum("eib,ekb->eik", factors, selected, preferred_element_type=jnp.float32)
    summed = jnp.einsum("ep,eik->pik", pair_pick, back_terms, precision=highest)
    summed = summed.reshape(panel_count, target_count, rank_dim, rank_dim)
    middle_terms = jnp.einsum("dtik,dij->dtkj", summed, coupling, precision=highest)
    partial_rows = jnp.einsum(
        "dtkj,djb->tkb", middle_terms, gathered.astype(jnp.float32), precision=highest
    )
    coeff_part = wide_reduce(partial_rows, wide_count)
    root_width = math.sqrt(full_width)
    return (own_basis * root_width, coeff_part / root_width)


def eliminate(gram):
    size = gram.shape[0]
    step = 8
    lane = lax.broadcasted_iota(jnp.int32, (size, size), 1)
    line = lax.broadcasted_iota(jnp.int32, (size, size), 0)
    eye = jnp.where(lane == line, 1.0, 0.0).astype(jnp.float32)
    whole = jnp.concatenate([gram, eye], axis=1)
    groups = [whole[r : r + step] for r in range(0, size, step)]
    for top, group in enumerate(groups):
        first = top * step
        rows = [group[p : p + 1] for p in range(step)]
        block = [
            [jnp.broadcast_to(row[:, first + q : first + q + 1], row.shape) for q in range(step)]
            for row in rows
        ]
        inverse = []
        ratio = {}
        for p in range(step):
            inverse.append(1.0 / block[p][p])
            for q in range(p + 1, step):
                ratio[p, q] = block[p][q] * inverse[p]
                rows[q] = rows[q] - ratio[p, q] * rows[p]
                for s in range(q, step):
                    block[q][s] = block[q][s] - ratio[p, q] * block[p][s]
        solved = [None] * step
        for p in reversed(range(step)):
            solved[p] = rows[p] * inverse[p]
            for q in range(p + 1, step):
                solved[p] = solved[p] - ratio[p, q] * solved[q]
        groups[top] = jnp.concatenate(rows, axis=0)
        for r in range(top + 1, size // step):
            change = groups[r][:, first : first + 1] * solved[0]
            for p in range(1, step):
                change = change + groups[r][:, first + p : first + p + 1] * solved[p]
            groups[r] = groups[r] - change
    whole = jnp.concatenate(groups, axis=0)
    pivots = jnp.sum(jnp.where(lane == line, whole[:, :size], 0.0), axis=1, keepdims=True)
    return whole[:, size:] * (1.0 / jnp.sqrt(pivots))


def entry_order(panel, target, count, panels):
    slots = panel.shape[1]
    shape = (slots, slots)
    lane = lax.broadcasted_iota(jnp.int32, shape, 1)
    line = lax.broadcasted_iota(jnp.int32, shape, 0)
    across = jnp.where(lane[:1] < count, target * panels + panel, slots * panels)
    key = jnp.sum(jnp.where(line == lane, across, 0), axis=1, keepdims=True)
    ahead = (across < key) | ((across == key) & (lane < line))
    place = jnp.sum(ahead.astype(jnp.int32), axis=1, keepdims=True)
    order = jnp.sum(jnp.where(place == lane, line, 0), axis=0, keepdims=True)
    here = jnp.sum(jnp.where(place == lane, key + 1, 0), axis=0, keepdims=True)
    before = jnp.sum(jnp.where(place + 1 == lane, key + 1, 0), axis=0, keepdims=True)
    keep = (here == before).astype(jnp.int32)
    upto = jnp.sum((key <= lane).astype(jnp.int32), axis=0, keepdims=True)
    some = jnp.sum((key == lane).astype(jnp.int32), axis=0, keepdims=True)
    last = jnp.where(some > 0, upto - 1, slots)
    return order, keep, last


def recompress(
    f_hbm, panel_hbm, target_hbm, count_hbm, s_hbm, c_hbm, p_hbm, left, right,
    panel, target, count, order_vec, meta, coup, cbd, fbuf, cum, pbuf, sfull, scol, coef, ysend, yrecv, zsend, zrecv, total, qall, midall,
    loc_sem, small_sem, s_send, s_recv, c_send, c_recv, g_send, g_recv, y_sem, yr_sem, z_sem, zr_sem,
    q_send, q_recv, m_send, m_recv,
):
    slots = f_hbm.shape[0]
    rank = f_hbm.shape[2]
    width = f_hbm.shape[3]
    quarter = width // NARROW
    share = width // WAYS
    w = lax.axis_index("wide")
    n = lax.axis_index("narrow")
    z, y = w // YWAY, w % YWAY
    flip = w + 1 - 2 * y

    def zflip(m):
        return (z, z + 1 - 2 * (z % 2), (z + 2) % 4, 3 - z)[m]

    def remote(src, dst, send, recv, wide_at, narrow_at):
        return pltpu.make_async_remote_copy(
            src_ref=src, dst_ref=dst, send_sem=send, recv_sem=recv,
            device_id=(wide_at, narrow_at), device_id_type=pl.DeviceIdType.MESH,
        )

    barrier = pltpu.get_barrier_semaphore()
    for k in range(1, NARROW):
        pl.semaphore_signal(
            barrier, inc=1, device_id=(w, (n + k) % NARROW), device_id_type=pl.DeviceIdType.MESH
        )
    for k in range(1, WAYS):
        pl.semaphore_signal(
            barrier, inc=1, device_id=((w + k) % WAYS, n), device_id_type=pl.DeviceIdType.MESH
        )

    smalls = [
        pltpu.make_async_copy(src, dst, small_sem.at[i])
        for i, (src, dst) in enumerate(
            ((panel_hbm, panel), (target_hbm, target), (count_hbm, count), (c_hbm, coup))
        )
    ]
    step = slots // FSPLIT
    loads = [
        pltpu.make_async_copy(
            f_hbm.at[pl.ds(i * step, step)], fbuf.at[pl.ds(i * step, step)], loc_sem.at[i]
        )
        for i in range(FSPLIT)
    ]
    own_s = pltpu.make_async_copy(s_hbm, sfull.at[n], loc_sem.at[FSPLIT])
    load_p = pltpu.make_async_copy(p_hbm, pbuf, loc_sem.at[FSPLIT + 1])
    for c in smalls:
        c.start()
    own_s.start()
    for c in loads:
        c.start()
    load_p.start()

    pl.semaphore_wait(barrier, NARROW + WAYS - 2)

    twin, across = n + 1 - 2 * (n % 2), (n + 2) % NARROW
    twin_across = (twin + 2) % NARROW
    sent = []

    def s_send_to(src, ref, sem, to):
        c = remote(src, ref, s_send.at[sem], s_recv.at[sem], w, to)
        c.start()
        sent.append(c)

    def s_wait(ref, sem):
        remote(ref, ref, s_send.at[sem], s_recv.at[sem], w, twin).wait_recv()

    for p in range(coup.shape[0]):
        s_send_to(s_hbm.at[p], sfull.at[n, p], 3 * p, across)
        s_send_to(s_hbm.at[p], sfull.at[n, p], 3 * p + 1, twin)
    for c in smalls:
        c.wait()
    order_vec[...] = jnp.zeros(order_vec.shape, jnp.int32)
    for i, row in enumerate(entry_order(panel[...], target[...], count[...], coup.shape[0])):
        order_vec[i : i + 1, :slots] = row
    meta_copy = pltpu.make_async_copy(order_vec, meta, small_sem.at[4])
    meta_copy.start()
    empty = jnp.zeros((rank, rank), jnp.float32)
    cbd[:rank] = jnp.concatenate([coup[0], empty], axis=1)
    cbd[rank:] = jnp.concatenate([empty, coup[1]], axis=1)
    for p in range(coup.shape[0]):
        s_wait(sfull.at[across, p], 3 * p)
        s_send_to(sfull.at[across, p], sfull.at[across, p], 3 * p + 2, twin)

    cum[slots] = jnp.zeros((2, rank, width), jnp.bfloat16)
    meta_copy.wait()
    for c in loads:
        c.wait()
    for c0 in range(0, rank, 16):

        def add(s, acc):
            x = fbuf[meta[0, s], 0, pl.ds(c0, 16), :].astype(jnp.float32)
            acc = acc * meta[1, s].astype(jnp.float32) + x
            high = acc.astype(jnp.bfloat16)
            cum[s, 0, pl.ds(c0, 16), :] = high
            cum[s, 1, pl.ds(c0, 16), :] = (acc - high.astype(jnp.float32)).astype(jnp.bfloat16)
            return acc

        lax.fori_loop(0, slots, add, jnp.zeros((16, width), jnp.float32), unroll=2)

    def pair_rows(t):
        first, second = meta[2, 2 * t], meta[2, 2 * t + 1]
        return jnp.concatenate(
            [cum[first, 0], cum[second, 0], cum[first, 1], cum[second, 1]], axis=0
        )

    load_p.wait()
    own_s.wait()

    def project(at):
        cols = pl.ds(pl.multiple_of(at * quarter, quarter), quarter)
        probe = pbuf[:, :, cols].reshape(-1, quarter)
        return lax.dot_general(
            probe, sfull[at].reshape(-1, quarter), LAST_DIMS, preferred_element_type=jnp.float32
        )

    projected = project(n)
    projected = projected + project(across)
    for at, sem in ((twin, 1), (twin_across, 2)):
        for p in range(coup.shape[0]):
            s_wait(sfull.at[at, p], 3 * p + sem)
        projected = projected + project(at)
    coef[...] = lax.dot_general(
        projected, cbd[...], LAST_DIMS, precision=HIGHEST, preferred_element_type=jnp.float32
    ).astype(jnp.bfloat16)

    def partial_sketch(t):
        lhs = coef[pl.ds(pl.multiple_of(t * rank, rank), rank), :]
        lhs = jnp.concatenate([lhs, lhs], axis=1)
        return jnp.dot(lhs, pair_rows(t), preferred_element_type=jnp.float32)

    order = (2, 3, 1, 0)
    cut = rank // RCUT
    y_copies, z_copies = {}, {}

    def y_stage(k):
        ysend[k] = partial_sketch(zflip(order[k]) * YWAY + (1 - y)).astype(jnp.bfloat16)
        for h in range(RCUT):
            at = pl.ds(h * cut, cut)
            c = remote(
                ysend.at[k, at], yrecv.at[k, at], y_sem.at[k, h], yr_sem.at[k, h], flip, n
            )
            c.start()
            sent.append(c)
            y_copies[k, h] = c

    def z_stage(k):
        to = zflip(order[k]) * YWAY + y
        own = partial_sketch(to)
        for h in range(RCUT):
            at = pl.ds(h * cut, cut)
            y_copies[k, h].wait_recv()
            summed = own[h * cut : (h + 1) * cut] + yrecv[k, at].astype(jnp.float32)
            if order[k]:
                zsend[k, at] = summed.astype(jnp.bfloat16)
                c = remote(
                    zsend.at[k, at], zrecv.at[k, at], z_sem.at[k, h], zr_sem.at[k, h], to, n
                )
                c.start()
                sent.append(c)
                z_copies[k, h] = c
            else:
                total[at] = summed

    y_stage(0)
    y_stage(1)
    for k in range(ZWAY):
        if k + 2 < ZWAY:
            y_stage(k + 2)
        z_stage(k)
    for k in (2, 0, 1):
        for h in range(RCUT):
            at = pl.ds(h * cut, cut)
            z_copies[k, h].wait_recv()
            total[at] += zrecv[k, at].astype(jnp.float32)

    part = rank // 2

    def s_part(to):
        cols = pl.ds(pl.multiple_of((to % 2) * share, share), share)
        rows = pl.ds(pl.multiple_of((n % 2) * part, part), part)
        return sfull.at[to // 2, n // 2, rows, cols]

    for k in range(1, WAYS):
        to = (w + k) % WAYS
        c = remote(s_part(to), scol.at[n, w], c_send.at[k], c_recv.at[k], to, n)
        c.start()
        sent.append(c)
    scol[n, w] = s_part(w)[...]

    sketch = total[...]
    gram = lax.dot_general(
        sketch, sketch, LAST_DIMS, precision=HIGHEST, preferred_element_type=jnp.float32
    )
    inverse = eliminate(gram)
    qall[w] = jnp.dot(
        inverse, sketch, precision=HIGHEST, preferred_element_type=jnp.float32
    ).astype(jnp.bfloat16)

    def middle(t):
        terms = lax.dot_general(
            qall[t], pair_rows(t), LAST_DIMS, preferred_element_type=jnp.float32
        )
        terms = terms[:, : 2 * rank] + terms[:, 2 * rank :]
        rows = jnp.dot(terms, cbd[...], precision=HIGHEST, preferred_element_type=jnp.float32)
        midall[w, pl.ds(pl.multiple_of(t * rank, rank), rank), :] = rows.astype(jnp.bfloat16)

    def arrivals(at):
        return (at, at + 1 - 2 * (at % 2), 2 - at // 2, 3 - 3 * (at // 2))

    inner = z % 3 != 0
    later = []

    def start(c, holds=None):
        if holds is None:
            c.start()
        else:
            pl.when(holds)(c.start)
        later.append((c, holds))

    def spread(ref, send, recv):
        start(remote(ref, ref, send(1), recv(z), (z + 1) % 4 * YWAY + y, n), z < ZWAY - 1)
        start(remote(ref, ref, send(2), recv(z), (z + 3) % 4 * YWAY + y, n), z > 0)
        start(remote(ref, ref, send(0), recv(ZWAY + z), flip, n))

    def pass_on(ref, j, src_z, send, recv, line=True):
        remote(ref, ref, send(0), recv(src_z), w, n).wait_recv()
        if line:
            to = (3 - z if j == 1 else (3 * z + 1) % 4) * YWAY + y
            start(remote(ref, ref, send(1 + 2 * j), recv(src_z), to, n), inner)
        start(remote(ref, ref, send(2 + 2 * j), recv(ZWAY + src_z), flip, n))

    def spread_straight(ref, send, recv, all_y):
        start(remote(ref, ref, send(0), recv(ZWAY + z), flip, n))
        for k, src_z in enumerate(arrivals(z)):
            if k:
                start(remote(ref, ref, send(k), recv(z), src_z * YWAY + y, n))
        for k, src_z in enumerate(arrivals(z)):
            if k and all_y:
                to = src_z * YWAY + 1 - y
                start(remote(ref, ref, send(3 + k), recv(ZWAY + z), to, n))

    def take(ref, src_z, send, recv):
        remote(ref, ref, send(0), recv(ZWAY + src_z), w, n).wait_recv()

    def q_sems(h):
        return (lambda k: q_send.at[h, k]), (lambda k: q_recv.at[h, k])

    def q_piece(at, h):
        return qall.at[at, pl.ds(h * (rank // QCUT), rank // QCUT), :]

    def mid_sems(i):
        return (lambda k: m_send.at[i, k]), (lambda k: m_recv.at[i, k])

    def mid_piece(src_z, src_y, i):
        first = arrivals(src_z)[i] * YWAY * rank
        rows = pl.ds(pl.multiple_of(first, YWAY * rank), YWAY * rank)
        return midall.at[src_z * YWAY + src_y, rows, :]

    for h in range(QCUT):
        spread(q_piece(w, h), *q_sems(h))
    middle(w)
    for k in range(1, WAYS):
        src = scol.at[n, (w + WAYS - k) % WAYS]
        remote(src, src, c_send.at[k], c_recv.at[k], w, twin).wait_recv()
    for k in range(1, NARROW):
        c = remote(
            scol.at[n], scol.at[n], g_send.at[k], g_recv.at[k], w, (n + k) % NARROW
        )
        c.start()
        sent.append(c)

    def far_half(j):
        src_z = arrivals(z)[j]
        far = src_z * YWAY + 1 - y
        for h in range(QCUT):
            take(q_piece(far, h), src_z, *q_sems(h))
        middle(far)
        if ROUTES[j] == "L":
            spread(mid_piece(z, y, j), *mid_sems(j))
        else:
            spread_straight(mid_piece(z, y, j), *mid_sems(j), ROUTES[j] == "F")

    def row_start(i):
        piece = mid_piece(z, 1 - y, i)
        send, recv = mid_sems(i)
        take(piece, z, send, recv)
        for k, src_z in enumerate(arrivals(z)):
            if k:
                start(remote(piece, piece, send(3 + k), recv(ZWAY + z), src_z * YWAY + y, n))

    def mid_pass(i, j):
        src_z = arrivals(z)[j]
        piece = mid_piece(src_z, y, i)
        send, recv = mid_sems(i)
        if ROUTES[i] in "FS":
            remote(piece, piece, send(0), recv(src_z), w, n).wait_recv()
        else:
            pass_on(piece, j, src_z, send, recv, ROUTES[i] == "L")

    for j in range(1, ZWAY):
        src_z = arrivals(z)[j]
        near = src_z * YWAY + y
        for h in range(QCUT):
            pass_on(q_piece(near, h), j, src_z, *q_sems(h))
        far_half(j - 1)
        middle(near)
    if ROUTES[0] == "S":
        row_start(0)
    for j in range(1, ZWAY):
        mid_pass(0, j)
    if ROUTES[1] == "S":
        row_start(1)
    far_half(ZWAY - 1)
    if ROUTES[2] == "S":
        row_start(2)
    for i in range(1, ZWAY):
        for j in range(1, ZWAY):
            mid_pass(i, j)

    for k in range(WAYS):
        cols = pl.ds(pl.multiple_of(w * share, share), share)
        left[k] = qall[k, :, cols]

    def rows_of(src):
        shared = jnp.concatenate([scol[k, src] for k in range(NARROW)], axis=0)
        return jnp.dot(midall[src], shared, preferred_element_type=jnp.float32)

    for k in range(1, NARROW):
        src = scol.at[(n + NARROW - k) % NARROW]
        remote(src, src, g_send.at[k], g_recv.at[k], w, twin).wait_recv()
    rows = rows_of(w)
    for j, src_z in enumerate(arrivals(z)):
        if j:
            rows = rows + rows_of(src_z * YWAY + y)
    for j, src_z in enumerate(arrivals(z)):
        for i in range(ZWAY):
            if ROUTES[i] != "S" or j:
                take(mid_piece(src_z, 1 - y, i), src_z, *mid_sems(i))
        rows = rows + rows_of(src_z * YWAY + 1 - y)
    right[...] = rows.reshape(right.shape)
    for c in sent:
        c.wait_send()
    for c, holds in later:
        if holds is None:
            c.wait_send()
        else:
            pl.when(holds)(c.wait_send)


def fused(entry_factor, entry_panel, entry_target, entry_count, panel_shared, coupling, probes):
    slots, _, rank, width = entry_factor.shape
    panels = panel_shared.shape[0]
    targets = probes.shape[0]
    share = width // WAYS
    depth = panels * rank
    bf16, f32, i32 = jnp.bfloat16, jnp.float32, jnp.int32
    dma = pltpu.SemaphoreType.DMA
    left, right = pl.pallas_call(
        recompress,
        out_shape=(
            jax.ShapeDtypeStruct((targets, rank, share), bf16),
            jax.ShapeDtypeStruct((targets, rank, share), f32),
        ),
        in_specs=[pl.BlockSpec(memory_space=pltpu.HBM)] * 7,
        out_specs=(
            pl.BlockSpec(memory_space=pltpu.VMEM),
            pl.BlockSpec(memory_space=pltpu.VMEM),
        ),
        scratch_shapes=[
            pltpu.VMEM((1, slots), i32),
            pltpu.VMEM((1, slots), i32),
            pltpu.VMEM((1, 1), i32),
            pltpu.VMEM((8, 128), i32),
            pltpu.SMEM((8, 128), i32),
            pltpu.VMEM((panels, rank, rank), f32),
            pltpu.VMEM((depth, depth), f32),
            pltpu.VMEM((slots, 1, rank, width), bf16),
            pltpu.VMEM((slots + 1, 2, rank, width), bf16),
            pltpu.VMEM((targets, rank, width), bf16),
            pltpu.VMEM((NARROW, panels, rank, width // NARROW), bf16),
            pltpu.VMEM((NARROW, WAYS, depth // NARROW, share), bf16),
            pltpu.VMEM((targets * rank, depth), bf16),
            pltpu.VMEM((ZWAY, rank, width), bf16),
            pltpu.VMEM((ZWAY, rank, width), bf16),
            pltpu.VMEM((ZWAY - 1, rank, width), bf16),
            pltpu.VMEM((ZWAY - 1, rank, width), bf16),
            pltpu.VMEM((rank, width), f32),
            pltpu.VMEM((targets, rank, width), bf16),
            pltpu.VMEM((WAYS, targets * rank, depth), bf16),
            dma((FSPLIT + 2,)),
            dma((5,)),
            dma((3 * panels,)),
            dma((3 * panels,)),
            dma((WAYS,)),
            dma((WAYS,)),
            dma((NARROW,)),
            dma((NARROW,)),
            dma((ZWAY, RCUT)),
            dma((ZWAY, RCUT)),
            dma((ZWAY, RCUT)),
            dma((ZWAY, RCUT)),
            dma((QCUT, 9)),
            dma((QCUT, WAYS)),
            dma((ZWAY, 9)),
            dma((ZWAY, WAYS)),
        ],
        compiler_params=pltpu.CompilerParams(
            collective_id=0, has_side_effects=True, vmem_limit_bytes=63 * 1024 * 1024
        ),
        name="recompress",
    )(entry_factor, entry_panel.T, entry_target.T, entry_count, panel_shared, coupling, probes)
    root_width = math.sqrt(width)
    return (left.astype(f32) * root_width, right / root_width)


def solution(mesh):
    placed = (
        P("wide", "narrow", None, None),
        P("wide", "narrow"),
        P("wide", "narrow"),
        P("narrow", "wide"),
        P("wide", None, "narrow"),
        P("wide", None, None),
        P("narrow", None, None),
    )
    return jax.shard_map(
        fused if mesh.shape["wide"] == WAYS and mesh.shape["narrow"] == NARROW else shards,
        mesh=mesh,
        in_specs=placed,
        out_specs=(P("narrow", None, "wide"), P("narrow", None, "wide")),
        check_vma=False,
    )
```

```python
import functools
import math

import jax
import jax.numpy as jnp
from jax import lax
from jax.experimental import pallas as pl
from jax.experimental.pallas import tpu as pltpu
from jax.sharding import PartitionSpec as P

HIGHEST = lax.Precision.HIGHEST
LAST_DIMS = (((1,), (1,)), ((), ()))
ZWAY = 4
YWAY = 2
WAYS = ZWAY * YWAY
NARROW = 4
FSPLIT = 4
RCUT = 4
QCUT = 4
ROUTES = "LDDD"

def wide_reduce(x, count):
    lead, rows, width = x.shape
    pieces = x.reshape(lead, rows, count, width // count).transpose(2, 0, 1, 3)
    pieces = lax.all_to_all(pieces, "wide", 0, 0, tiled=True)
    return pieces.sum(axis=0)


def wide_gather(x, count):
    lead, rows, width = x.shape
    copies = jnp.broadcast_to(x[None], (count, lead, rows, width))
    copies = lax.all_to_all(copies, "wide", 0, 0, tiled=True)
    return copies.transpose(1, 2, 0, 3).reshape(lead, rows, count * width)


def lower_inverse(lower):
    highest = lax.Precision.HIGHEST
    size = lower.shape[-1]
    eye = jnp.eye(size, dtype=lower.dtype)
    diag = jnp.diagonal(lower, axis1=-2, axis2=-1)
    strict = eye - lower / diag[..., :, None]
    unit_inverse = eye + strict
    power = strict
    for _ in range(max(size - 1, 1).bit_length() - 1):
        power = jnp.einsum("tij,tjk->tik", power, power, precision=highest)
        unit_inverse = unit_inverse + jnp.einsum(
            "tij,tjk->tik", unit_inverse, power, precision=highest
        )
    return unit_inverse / diag[..., None, :]


def shards(entry_factor, entry_panel, entry_target, entry_count, panel_shared, coupling, probes):
    highest = lax.Precision.HIGHEST
    factors = entry_factor[:, 0]
    slot_count = factors.shape[0]
    rank_dim = factors.shape[1]
    full_width = factors.shape[2]
    panel_count = panel_shared.shape[0]
    target_count = probes.shape[0]
    live_mask = (jnp.arange(slot_count) < entry_count[0, 0]).astype(jnp.float32)
    pick_panel = (entry_panel == jnp.arange(panel_count)[None, :]).astype(jnp.float32) * live_mask[
        :, None
    ]
    pick_target = (entry_target == jnp.arange(target_count)[None, :]).astype(jnp.float32)
    pair_pick = (pick_panel[:, :, None] * pick_target[:, None, :]).reshape(
        slot_count, panel_count * target_count
    )
    gathered = lax.all_gather(panel_shared, "narrow", axis=2, tiled=True)
    projected = jnp.einsum("drb,tkb->dtrk", gathered, probes, preferred_element_type=jnp.float32)
    coefficients = jnp.einsum("dij,dtjk->dtik", coupling, projected, precision=highest).astype(
        jnp.bfloat16
    )
    coeff_table = coefficients.reshape(panel_count * target_count, rank_dim * rank_dim)
    chosen = jnp.dot(
        pair_pick.astype(jnp.bfloat16), coeff_table, preferred_element_type=jnp.float32
    )
    chosen = chosen.astype(jnp.bfloat16).reshape(slot_count, rank_dim, rank_dim)
    contributions = jnp.einsum("eji,ejb->eib", chosen, factors, preferred_element_type=jnp.float32)
    sketch = jnp.einsum("et,eib->tib", pick_target, contributions, precision=highest)
    wide_count = lax.axis_size("wide")
    share_cols = full_width // wide_count
    sketch_own = wide_reduce(sketch, wide_count)
    gram_part = jnp.einsum("tib,tjb->tij", sketch_own, sketch_own, precision=highest)
    gram_copies = jnp.broadcast_to(gram_part[None], (wide_count,) + gram_part.shape)
    gram_matrix = lax.all_to_all(gram_copies, "wide", 0, 0, tiled=True).sum(axis=0)
    sketch_sum = wide_gather(sketch_own, wide_count)
    lower_factor = jnp.linalg.cholesky(gram_matrix)
    basis = jnp.einsum(
        "tij,tjb->tib", lower_inverse(lower_factor), sketch_sum, precision=highest
    )
    basis_round = basis.astype(jnp.bfloat16)
    own_basis = lax.dynamic_slice_in_dim(basis, lax.axis_index("wide") * share_cols, share_cols, 2)
    selected = jnp.einsum(
        "et,tkb->ekb",
        pick_target.astype(jnp.bfloat16),
        basis_round,
        preferred_element_type=jnp.float32,
    )
    selected = selected.astype(jnp.bfloat16)
    back_terms = jnp.einsum("eib,ekb->eik", factors, selected, preferred_element_type=jnp.float32)
    summed = jnp.einsum("ep,eik->pik", pair_pick, back_terms, precision=highest)
    summed = summed.reshape(panel_count, target_count, rank_dim, rank_dim)
    middle_terms = jnp.einsum("dtik,dij->dtkj", summed, coupling, precision=highest)
    partial_rows = jnp.einsum(
        "dtkj,djb->tkb", middle_terms, gathered.astype(jnp.float32), precision=highest
    )
    coeff_part = wide_reduce(partial_rows, wide_count)
    root_width = math.sqrt(full_width)
    return (own_basis * root_width, coeff_part / root_width)


def eliminate(gram):
    size = gram.shape[0]
    step = 8
    lane = lax.broadcasted_iota(jnp.int32, (size, size), 1)
    line = lax.broadcasted_iota(jnp.int32, (size, size), 0)
    eye = jnp.where(lane == line, 1.0, 0.0).astype(jnp.float32)
    whole = jnp.concatenate([gram, eye], axis=1)
    groups = [whole[r : r + step] for r in range(0, size, step)]
    for top, group in enumerate(groups):
        first = top * step
        rows = [group[p : p + 1] for p in range(step)]
        block = [
            [jnp.broadcast_to(row[:, first + q : first + q + 1], row.shape) for q in range(step)]
            for row in rows
        ]
        inverse = []
        ratio = {}
        for p in range(step):
            inverse.append(1.0 / block[p][p])
            for q in range(p + 1, step):
                ratio[p, q] = block[p][q] * inverse[p]
                rows[q] = rows[q] - ratio[p, q] * rows[p]
                for s in range(q, step):
                    block[q][s] = block[q][s] - ratio[p, q] * block[p][s]
        solved = [None] * step
        for p in reversed(range(step)):
            solved[p] = rows[p] * inverse[p]
            for q in range(p + 1, step):
                solved[p] = solved[p] - ratio[p, q] * solved[q]
        groups[top] = jnp.concatenate(rows, axis=0)
        for r in range(top + 1, size // step):
            change = groups[r][:, first : first + 1] * solved[0]
            for p in range(1, step):
                change = change + groups[r][:, first + p : first + p + 1] * solved[p]
            groups[r] = groups[r] - change
    whole = jnp.concatenate(groups, axis=0)
    pivots = jnp.sum(jnp.where(lane == line, whole[:, :size], 0.0), axis=1, keepdims=True)
    return whole[:, size:] * (1.0 / jnp.sqrt(pivots))


def entry_order(panel, target, count, panels):
    slots = panel.shape[1]
    shape = (slots, slots)
    lane = lax.broadcasted_iota(jnp.int32, shape, 1)
    line = lax.broadcasted_iota(jnp.int32, shape, 0)
    across = jnp.where(lane[:1] < count, target * panels + panel, slots * panels)
    key = jnp.sum(jnp.where(line == lane, across, 0), axis=1, keepdims=True)
    ahead = (across < key) | ((across == key) & (lane < line))
    place = jnp.sum(ahead.astype(jnp.int32), axis=1, keepdims=True)
    order = jnp.sum(jnp.where(place == lane, line, 0), axis=0, keepdims=True)
    here = jnp.sum(jnp.where(place == lane, key + 1, 0), axis=0, keepdims=True)
    before = jnp.sum(jnp.where(place + 1 == lane, key + 1, 0), axis=0, keepdims=True)
    keep = (here == before).astype(jnp.int32)
    upto = jnp.sum((key <= lane).astype(jnp.int32), axis=0, keepdims=True)
    some = jnp.sum((key == lane).astype(jnp.int32), axis=0, keepdims=True)
    last = jnp.where(some > 0, upto - 1, slots)
    return order, keep, last


def recompress(
    f_hbm, panel_hbm, target_hbm, count_hbm, s_hbm, c_hbm, p_hbm, left, right,
    panel, target, count, order_vec, meta, coup, cbd, fbuf, cum, pbuf, sfull, scol, coef, ysend, yrecv, zsend, zrecv, total, qall, midall,
    loc_sem, small_sem, s_send, s_recv, c_send, c_recv, g_send, g_recv, y_sem, yr_sem, z_sem, zr_sem,
    q_send, q_recv, m_send, m_recv,
):
    slots = f_hbm.shape[0]
    rank = f_hbm.shape[2]
    width = f_hbm.shape[3]
    quarter = width // NARROW
    share = width // WAYS
    w = lax.axis_index("wide")
    n = lax.axis_index("narrow")
    z, y = w // YWAY, w % YWAY
    flip = w + 1 - 2 * y

    def zflip(m):
        return (z, z + 1 - 2 * (z % 2), (z + 2) % 4, 3 - z)[m]

    def remote(src, dst, send, recv, wide_at, narrow_at):
        return pltpu.make_async_remote_copy(
            src_ref=src, dst_ref=dst, send_sem=send, recv_sem=recv,
            device_id=(wide_at, narrow_at), device_id_type=pl.DeviceIdType.MESH,
        )

    barrier = pltpu.get_barrier_semaphore()
    for k in range(1, NARROW):
        pl.semaphore_signal(
            barrier, inc=1, device_id=(w, (n + k) % NARROW), device_id_type=pl.DeviceIdType.MESH
        )
    for k in range(1, WAYS):
        pl.semaphore_signal(
            barrier, inc=1, device_id=((w + k) % WAYS, n), device_id_type=pl.DeviceIdType.MESH
        )

    smalls = [
        pltpu.make_async_copy(src, dst, small_sem.at[i])
        for i, (src, dst) in enumerate(
            ((panel_hbm, panel), (target_hbm, target), (count_hbm, count), (c_hbm, coup))
        )
    ]
    step = slots // FSPLIT
    loads = [
        pltpu.make_async_copy(
            f_hbm.at[pl.ds(i * step, step)], fbuf.at[pl.ds(i * step, step)], loc_sem.at[i]
        )
        for i in range(FSPLIT)
    ]
    own_s = pltpu.make_async_copy(s_hbm, sfull.at[n], loc_sem.at[FSPLIT])
    load_p = pltpu.make_async_copy(p_hbm, pbuf, loc_sem.at[FSPLIT + 1])
    for c in smalls:
        c.start()
    own_s.start()
    for c in loads:
        c.start()
    load_p.start()

    pl.semaphore_wait(barrier, NARROW + WAYS - 2)

    twin, across = n + 1 - 2 * (n % 2), (n + 2) % NARROW
    twin_across = (twin + 2) % NARROW
    sent = []

    def s_send_to(src, ref, sem, to):
        c = remote(src, ref, s_send.at[sem], s_recv.at[sem], w, to)
        c.start()
        sent.append(c)

    def s_wait(ref, sem):
        remote(ref, ref, s_send.at[sem], s_recv.at[sem], w, twin).wait_recv()

    for p in range(coup.shape[0]):
        s_send_to(s_hbm.at[p], sfull.at[n, p], 3 * p, across)
        s_send_to(s_hbm.at[p], sfull.at[n, p], 3 * p + 1, twin)
    for c in smalls:
        c.wait()
    order_vec[...] = jnp.zeros(order_vec.shape, jnp.int32)
    for i, row in enumerate(entry_order(panel[...], target[...], count[...], coup.shape[0])):
        order_vec[i : i + 1, :slots] = row
    meta_copy = pltpu.make_async_copy(order_vec, meta, small_sem.at[4])
    meta_copy.start()
    empty = jnp.zeros((rank, rank), jnp.float32)
    cbd[:rank] = jnp.concatenate([coup[0], empty], axis=1)
    cbd[rank:] = jnp.concatenate([empty, coup[1]], axis=1)
    for p in range(coup.shape[0]):
        s_wait(sfull.at[across, p], 3 * p)
        s_send_to(sfull.at[across, p], sfull.at[across, p], 3 * p + 2, twin)

    cum[slots] = jnp.zeros((2, rank, width), jnp.bfloat16)
    meta_copy.wait()
    for c in loads:
        c.wait()
    for c0 in range(0, rank, 16):

        def add(s, acc):
            x = fbuf[meta[0, s], 0, pl.ds(c0, 16), :].astype(jnp.float32)
            acc = acc * meta[1, s].astype(jnp.float32) + x
            high = acc.astype(jnp.bfloat16)
            cum[s, 0, pl.ds(c0, 16), :] = high
            cum[s, 1, pl.ds(c0, 16), :] = (acc - high.astype(jnp.float32)).astype(jnp.bfloat16)
            return acc

        lax.fori_loop(0, slots, add, jnp.zeros((16, width), jnp.float32), unroll=2)

    def pair_rows(t):
        first, second = meta[2, 2 * t], meta[2, 2 * t + 1]
        return jnp.concatenate(
            [cum[first, 0], cum[second, 0], cum[first, 1], cum[second, 1]], axis=0
        )

    load_p.wait()
    own_s.wait()

    def project(at):
        cols = pl.ds(pl.multiple_of(at * quarter, quarter), quarter)
        probe = pbuf[:, :, cols].reshape(-1, quarter)
        return lax.dot_general(
            probe, sfull[at].reshape(-1, quarter), LAST_DIMS, preferred_element_type=jnp.float32
        )

    projected = project(n)
    projected = projected + project(across)
    for at, sem in ((twin, 1), (twin_across, 2)):
        for p in range(coup.shape[0]):
            s_wait(sfull.at[at, p], 3 * p + sem)
        projected = projected + project(at)
    coef[...] = lax.dot_general(
        projected, cbd[...], LAST_DIMS, precision=HIGHEST, preferred_element_type=jnp.float32
    ).astype(jnp.bfloat16)

    def partial_sketch(t):
        lhs = coef[pl.ds(pl.multiple_of(t * rank, rank), rank), :]
        lhs = jnp.concatenate([lhs, lhs], axis=1)
        return jnp.dot(lhs, pair_rows(t), preferred_element_type=jnp.float32)

    order = (2, 3, 1, 0)
    cut = rank // RCUT
    y_copies, z_copies = {}, {}

    def y_stage(k):
        ysend[k] = partial_sketch(zflip(order[k]) * YWAY + (1 - y)).astype(jnp.bfloat16)
        for h in range(RCUT):
            at = pl.ds(h * cut, cut)
            c = remote(
                ysend.at[k, at], yrecv.at[k, at], y_sem.at[k, h], yr_sem.at[k, h], flip, n
            )
            c.start()
            sent.append(c)
            y_copies[k, h] = c

    def z_stage(k):
        to = zflip(order[k]) * YWAY + y
        own = partial_sketch(to)
        for h in range(RCUT):
            at = pl.ds(h * cut, cut)
            y_copies[k, h].wait_recv()
            summed = own[h * cut : (h + 1) * cut] + yrecv[k, at].astype(jnp.float32)
            if order[k]:
                zsend[k, at] = summed.astype(jnp.bfloat16)
                c = remote(
                    zsend.at[k, at], zrecv.at[k, at], z_sem.at[k, h], zr_sem.at[k, h], to, n
                )
                c.start()
                sent.append(c)
                z_copies[k, h] = c
            else:
                total[at] = summed

    y_stage(0)
    y_stage(1)
    for k in range(ZWAY):
        if k + 2 < ZWAY:
            y_stage(k + 2)
        z_stage(k)
    for k in (2, 0, 1):
        for h in range(RCUT):
            at = pl.ds(h * cut, cut)
            z_copies[k, h].wait_recv()
            total[at] += zrecv[k, at].astype(jnp.float32)

    part = rank // 2

    def s_part(to):
        cols = pl.ds(pl.multiple_of((to % 2) * share, share), share)
        rows = pl.ds(pl.multiple_of((n % 2) * part, part), part)
        return sfull.at[to // 2, n // 2, rows, cols]

    for k in range(1, WAYS):
        to = (w + k) % WAYS
        c = remote(s_part(to), scol.at[n, w], c_send.at[k], c_recv.at[k], to, n)
        c.start()
        sent.append(c)
    scol[n, w] = s_part(w)[...]

    sketch = total[...]
    gram = lax.dot_general(
        sketch, sketch, LAST_DIMS, precision=HIGHEST, preferred_element_type=jnp.float32
    )
    inverse = eliminate(gram)
    qall[w] = jnp.dot(
        inverse, sketch, precision=HIGHEST, preferred_element_type=jnp.float32
    ).astype(jnp.bfloat16)

    def middle(t):
        terms = lax.dot_general(
            qall[t], pair_rows(t), LAST_DIMS, preferred_element_type=jnp.float32
        )
        terms = terms[:, : 2 * rank] + terms[:, 2 * rank :]
        rows = jnp.dot(terms, cbd[...], precision=HIGHEST, preferred_element_type=jnp.float32)
        midall[w, pl.ds(pl.multiple_of(t * rank, rank), rank), :] = rows.astype(jnp.bfloat16)

    def arrivals(at):
        return (at, at + 1 - 2 * (at % 2), 2 - at // 2, 3 - 3 * (at // 2))

    inner = z % 3 != 0
    later = []

    def start(c, holds=None):
        if holds is None:
            c.start()
        else:
            pl.when(holds)(c.start)
        later.append((c, holds))

    def spread(ref, send, recv):
        start(remote(ref, ref, send(1), recv(z), (z + 1) % 4 * YWAY + y, n), z < ZWAY - 1)
        start(remote(ref, ref, send(2), recv(z), (z + 3) % 4 * YWAY + y, n), z > 0)
        start(remote(ref, ref, send(0), recv(ZWAY + z), flip, n))

    def pass_on(ref, j, src_z, send, recv, line=True):
        remote(ref, ref, send(0), recv(src_z), w, n).wait_recv()
        if line:
            to = (3 - z if j == 1 else (3 * z + 1) % 4) * YWAY + y
            start(remote(ref, ref, send(1 + 2 * j), recv(src_z), to, n), inner)
        start(remote(ref, ref, send(2 + 2 * j), recv(ZWAY + src_z), flip, n))

    def spread_straight(ref, send, recv, all_y):
        start(remote(ref, ref, send(0), recv(ZWAY + z), flip, n))
        for k, src_z in enumerate(arrivals(z)):
            if k:
                start(remote(ref, ref, send(k), recv(z), src_z * YWAY + y, n))
        for k, src_z in enumerate(arrivals(z)):
            if k and all_y:
                to = src_z * YWAY + 1 - y
                start(remote(ref, ref, send(3 + k), recv(ZWAY + z), to, n))

    def take(ref, src_z, send, recv):
        remote(ref, ref, send(0), recv(ZWAY + src_z), w, n).wait_recv()

    def q_sems(h):
        return (lambda k: q_send.at[h, k]), (lambda k: q_recv.at[h, k])

    def q_piece(at, h):
        return qall.at[at, pl.ds(h * (rank // QCUT), rank // QCUT), :]

    def mid_sems(i):
        return (lambda k: m_send.at[i, k]), (lambda k: m_recv.at[i, k])

    def mid_piece(src_z, src_y, i):
        first = arrivals(src_z)[i] * YWAY * rank
        rows = pl.ds(pl.multiple_of(first, YWAY * rank), YWAY * rank)
        return midall.at[src_z * YWAY + src_y, rows, :]

    for h in range(QCUT):
        spread(q_piece(w, h), *q_sems(h))
    middle(w)
    def far_half(j):
        src_z = arrivals(z)[j]
        far = src_z * YWAY + 1 - y
        for h in range(QCUT):
            take(q_piece(far, h), src_z, *q_sems(h))
        middle(far)
        if ROUTES[j] == "L":
            spread(mid_piece(z, y, j), *mid_sems(j))
        else:
            spread_straight(mid_piece(z, y, j), *mid_sems(j), ROUTES[j] == "F")

    def row_start(i):
        piece = mid_piece(z, 1 - y, i)
        send, recv = mid_sems(i)
        take(piece, z, send, recv)
        for k, src_z in enumerate(arrivals(z)):
            if k:
                start(remote(piece, piece, send(3 + k), recv(ZWAY + z), src_z * YWAY + y, n))

    def mid_pass(i, j):
        src_z = arrivals(z)[j]
        piece = mid_piece(src_z, y, i)
        send, recv = mid_sems(i)
        if ROUTES[i] in "FS":
            remote(piece, piece, send(0), recv(src_z), w, n).wait_recv()
        else:
            pass_on(piece, j, src_z, send, recv, ROUTES[i] == "L")

    for j in range(1, ZWAY):
        src_z = arrivals(z)[j]
        near = src_z * YWAY + y
        for h in range(QCUT):
            pass_on(q_piece(near, h), j, src_z, *q_sems(h))
        far_half(j - 1)
        middle(near)
    for k in range(1, WAYS):
        src = scol.at[n, (w + WAYS - k) % WAYS]
        remote(src, src, c_send.at[k], c_recv.at[k], w, twin).wait_recv()
    for k in range(1, NARROW):
        c = remote(
            scol.at[n], scol.at[n], g_send.at[k], g_recv.at[k], w, (n + k) % NARROW
        )
        c.start()
        sent.append(c)

    if ROUTES[0] == "S":
        row_start(0)
    mid_pass(0, 1)
    if ROUTES[1] == "S":
        row_start(1)
    far_half(ZWAY - 1)
    if ROUTES[2] == "S":
        row_start(2)
    for i in range(ZWAY):
        for j in range(1, ZWAY):
            if i or j > 1:
                mid_pass(i, j)

    for k in range(WAYS):
        cols = pl.ds(pl.multiple_of(w * share, share), share)
        left[k] = qall[k, :, cols]

    def rows_of(src):
        shared = jnp.concatenate([scol[k, src] for k in range(NARROW)], axis=0)
        return jnp.dot(midall[src], shared, preferred_element_type=jnp.float32)

    for k in range(1, NARROW):
        src = scol.at[(n + NARROW - k) % NARROW]
        remote(src, src, g_send.at[k], g_recv.at[k], w, twin).wait_recv()
    rows = rows_of(w)
    for j, src_z in enumerate(arrivals(z)):
        if j:
            rows = rows + rows_of(src_z * YWAY + y)
    for j, src_z in enumerate(arrivals(z)):
        for i in range(ZWAY):
            if ROUTES[i] != "S" or j:
                take(mid_piece(src_z, 1 - y, i), src_z, *mid_sems(i))
        rows = rows + rows_of(src_z * YWAY + 1 - y)
    right[...] = rows.reshape(right.shape)
    for c in sent:
        c.wait_send()
    for c, holds in later:
        if holds is None:
            c.wait_send()
        else:
            pl.when(holds)(c.wait_send)


def fused(entry_factor, entry_panel, entry_target, entry_count, panel_shared, coupling, probes):
    slots, _, rank, width = entry_factor.shape
    panels = panel_shared.shape[0]
    targets = probes.shape[0]
    share = width // WAYS
    depth = panels * rank
    bf16, f32, i32 = jnp.bfloat16, jnp.float32, jnp.int32
    dma = pltpu.SemaphoreType.DMA
    left, right = pl.pallas_call(
        recompress,
        out_shape=(
            jax.ShapeDtypeStruct((targets, rank, share), bf16),
            jax.ShapeDtypeStruct((targets, rank, share), f32),
        ),
        in_specs=[pl.BlockSpec(memory_space=pltpu.HBM)] * 7,
        out_specs=(
            pl.BlockSpec(memory_space=pltpu.VMEM),
            pl.BlockSpec(memory_space=pltpu.VMEM),
        ),
        scratch_shapes=[
            pltpu.VMEM((1, slots), i32),
            pltpu.VMEM((1, slots), i32),
            pltpu.VMEM((1, 1), i32),
            pltpu.VMEM((8, 128), i32),
            pltpu.SMEM((8, 128), i32),
            pltpu.VMEM((panels, rank, rank), f32),
            pltpu.VMEM((depth, depth), f32),
            pltpu.VMEM((slots, 1, rank, width), bf16),
            pltpu.VMEM((slots + 1, 2, rank, width), bf16),
            pltpu.VMEM((targets, rank, width), bf16),
            pltpu.VMEM((NARROW, panels, rank, width // NARROW), bf16),
            pltpu.VMEM((NARROW, WAYS, depth // NARROW, share), bf16),
            pltpu.VMEM((targets * rank, depth), bf16),
            pltpu.VMEM((ZWAY, rank, width), bf16),
            pltpu.VMEM((ZWAY, rank, width), bf16),
            pltpu.VMEM((ZWAY - 1, rank, width), bf16),
            pltpu.VMEM((ZWAY - 1, rank, width), bf16),
            pltpu.VMEM((rank, width), f32),
            pltpu.VMEM((targets, rank, width), bf16),
            pltpu.VMEM((WAYS, targets * rank, depth), bf16),
            dma((FSPLIT + 2,)),
            dma((5,)),
            dma((3 * panels,)),
            dma((3 * panels,)),
            dma((WAYS,)),
            dma((WAYS,)),
            dma((NARROW,)),
            dma((NARROW,)),
            dma((ZWAY, RCUT)),
            dma((ZWAY, RCUT)),
            dma((ZWAY, RCUT)),
            dma((ZWAY, RCUT)),
            dma((QCUT, 9)),
            dma((QCUT, WAYS)),
            dma((ZWAY, 9)),
            dma((ZWAY, WAYS)),
        ],
        compiler_params=pltpu.CompilerParams(
            collective_id=0, has_side_effects=True, vmem_limit_bytes=63 * 1024 * 1024
        ),
        name="recompress",
    )(entry_factor, entry_panel.T, entry_target.T, entry_count, panel_shared, coupling, probes)
    root_width = math.sqrt(width)
    return (left.astype(f32) * root_width, right / root_width)


def solution(mesh):
    placed = (
        P("wide", "narrow", None, None),
        P("wide", "narrow"),
        P("wide", "narrow"),
        P("narrow", "wide"),
        P("wide", None, "narrow"),
        P("wide", None, None),
        P("narrow", None, None),
    )
    return jax.shard_map(
        fused if mesh.shape["wide"] == WAYS and mesh.shape["narrow"] == NARROW else shards,
        mesh=mesh,
        in_specs=placed,
        out_specs=(P("narrow", None, "wide"), P("narrow", None, "wide")),
        check_vma=False,
    )
```

```python
import functools
import math

import jax
import jax.numpy as jnp
from jax import lax
from jax.experimental import pallas as pl
from jax.experimental.pallas import tpu as pltpu
from jax.sharding import PartitionSpec as P

HIGHEST = lax.Precision.HIGHEST
LAST_DIMS = (((1,), (1,)), ((), ()))
ZWAY = 4
YWAY = 2
WAYS = ZWAY * YWAY
NARROW = 4
FSPLIT = 4
RCUT = 4
QCUT = 4
ROUTES = "LDDD"

def wide_reduce(x, count):
    lead, rows, width = x.shape
    pieces = x.reshape(lead, rows, count, width // count).transpose(2, 0, 1, 3)
    pieces = lax.all_to_all(pieces, "wide", 0, 0, tiled=True)
    return pieces.sum(axis=0)


def wide_gather(x, count):
    lead, rows, width = x.shape
    copies = jnp.broadcast_to(x[None], (count, lead, rows, width))
    copies = lax.all_to_all(copies, "wide", 0, 0, tiled=True)
    return copies.transpose(1, 2, 0, 3).reshape(lead, rows, count * width)


def lower_inverse(lower):
    highest = lax.Precision.HIGHEST
    size = lower.shape[-1]
    eye = jnp.eye(size, dtype=lower.dtype)
    diag = jnp.diagonal(lower, axis1=-2, axis2=-1)
    strict = eye - lower / diag[..., :, None]
    unit_inverse = eye + strict
    power = strict
    for _ in range(max(size - 1, 1).bit_length() - 1):
        power = jnp.einsum("tij,tjk->tik", power, power, precision=highest)
        unit_inverse = unit_inverse + jnp.einsum(
            "tij,tjk->tik", unit_inverse, power, precision=highest
        )
    return unit_inverse / diag[..., None, :]


def shards(entry_factor, entry_panel, entry_target, entry_count, panel_shared, coupling, probes):
    highest = lax.Precision.HIGHEST
    factors = entry_factor[:, 0]
    slot_count = factors.shape[0]
    rank_dim = factors.shape[1]
    full_width = factors.shape[2]
    panel_count = panel_shared.shape[0]
    target_count = probes.shape[0]
    live_mask = (jnp.arange(slot_count) < entry_count[0, 0]).astype(jnp.float32)
    pick_panel = (entry_panel == jnp.arange(panel_count)[None, :]).astype(jnp.float32) * live_mask[
        :, None
    ]
    pick_target = (entry_target == jnp.arange(target_count)[None, :]).astype(jnp.float32)
    pair_pick = (pick_panel[:, :, None] * pick_target[:, None, :]).reshape(
        slot_count, panel_count * target_count
    )
    gathered = lax.all_gather(panel_shared, "narrow", axis=2, tiled=True)
    projected = jnp.einsum("drb,tkb->dtrk", gathered, probes, preferred_element_type=jnp.float32)
    coefficients = jnp.einsum("dij,dtjk->dtik", coupling, projected, precision=highest).astype(
        jnp.bfloat16
    )
    coeff_table = coefficients.reshape(panel_count * target_count, rank_dim * rank_dim)
    chosen = jnp.dot(
        pair_pick.astype(jnp.bfloat16), coeff_table, preferred_element_type=jnp.float32
    )
    chosen = chosen.astype(jnp.bfloat16).reshape(slot_count, rank_dim, rank_dim)
    contributions = jnp.einsum("eji,ejb->eib", chosen, factors, preferred_element_type=jnp.float32)
    sketch = jnp.einsum("et,eib->tib", pick_target, contributions, precision=highest)
    wide_count = lax.axis_size("wide")
    share_cols = full_width // wide_count
    sketch_own = wide_reduce(sketch, wide_count)
    gram_part = jnp.einsum("tib,tjb->tij", sketch_own, sketch_own, precision=highest)
    gram_copies = jnp.broadcast_to(gram_part[None], (wide_count,) + gram_part.shape)
    gram_matrix = lax.all_to_all(gram_copies, "wide", 0, 0, tiled=True).sum(axis=0)
    sketch_sum = wide_gather(sketch_own, wide_count)
    lower_factor = jnp.linalg.cholesky(gram_matrix)
    basis = jnp.einsum(
        "tij,tjb->tib", lower_inverse(lower_factor), sketch_sum, precision=highest
    )
    basis_round = basis.astype(jnp.bfloat16)
    own_basis = lax.dynamic_slice_in_dim(basis, lax.axis_index("wide") * share_cols, share_cols, 2)
    selected = jnp.einsum(
        "et,tkb->ekb",
        pick_target.astype(jnp.bfloat16),
        basis_round,
        preferred_element_type=jnp.float32,
    )
    selected = selected.astype(jnp.bfloat16)
    back_terms = jnp.einsum("eib,ekb->eik", factors, selected, preferred_element_type=jnp.float32)
    summed = jnp.einsum("ep,eik->pik", pair_pick, back_terms, precision=highest)
    summed = summed.reshape(panel_count, target_count, rank_dim, rank_dim)
    middle_terms = jnp.einsum("dtik,dij->dtkj", summed, coupling, precision=highest)
    partial_rows = jnp.einsum(
        "dtkj,djb->tkb", middle_terms, gathered.astype(jnp.float32), precision=highest
    )
    coeff_part = wide_reduce(partial_rows, wide_count)
    root_width = math.sqrt(full_width)
    return (own_basis * root_width, coeff_part / root_width)


def eliminate(gram):
    size = gram.shape[0]
    step = 8
    lane = lax.broadcasted_iota(jnp.int32, (size, size), 1)
    line = lax.broadcasted_iota(jnp.int32, (size, size), 0)
    eye = jnp.where(lane == line, 1.0, 0.0).astype(jnp.float32)
    whole = jnp.concatenate([gram, eye], axis=1)
    groups = [whole[r : r + step] for r in range(0, size, step)]
    for top, group in enumerate(groups):
        first = top * step
        rows = [group[p : p + 1] for p in range(step)]
        block = [
            [jnp.broadcast_to(row[:, first + q : first + q + 1], row.shape) for q in range(step)]
            for row in rows
        ]
        inverse = []
        ratio = {}
        for p in range(step):
            inverse.append(1.0 / block[p][p])
            for q in range(p + 1, step):
                ratio[p, q] = block[p][q] * inverse[p]
                rows[q] = rows[q] - ratio[p, q] * rows[p]
                for s in range(q, step):
                    block[q][s] = block[q][s] - ratio[p, q] * block[p][s]
        solved = [None] * step
        for p in reversed(range(step)):
            solved[p] = rows[p] * inverse[p]
            for q in range(p + 1, step):
                solved[p] = solved[p] - ratio[p, q] * solved[q]
        groups[top] = jnp.concatenate(rows, axis=0)
        for r in range(top + 1, size // step):
            change = groups[r][:, first : first + 1] * solved[0]
            for p in range(1, step):
                change = change + groups[r][:, first + p : first + p + 1] * solved[p]
            groups[r] = groups[r] - change
    whole = jnp.concatenate(groups, axis=0)
    pivots = jnp.sum(jnp.where(lane == line, whole[:, :size], 0.0), axis=1, keepdims=True)
    return whole[:, size:] * (1.0 / jnp.sqrt(pivots))


def entry_order(panel, target, count, panels):
    slots = panel.shape[1]
    shape = (slots, slots)
    lane = lax.broadcasted_iota(jnp.int32, shape, 1)
    line = lax.broadcasted_iota(jnp.int32, shape, 0)
    across = jnp.where(lane[:1] < count, target * panels + panel, slots * panels)
    key = jnp.sum(jnp.where(line == lane, across, 0), axis=1, keepdims=True)
    ahead = (across < key) | ((across == key) & (lane < line))
    place = jnp.sum(ahead.astype(jnp.int32), axis=1, keepdims=True)
    order = jnp.sum(jnp.where(place == lane, line, 0), axis=0, keepdims=True)
    here = jnp.sum(jnp.where(place == lane, key + 1, 0), axis=0, keepdims=True)
    before = jnp.sum(jnp.where(place + 1 == lane, key + 1, 0), axis=0, keepdims=True)
    keep = (here == before).astype(jnp.int32)
    upto = jnp.sum((key <= lane).astype(jnp.int32), axis=0, keepdims=True)
    some = jnp.sum((key == lane).astype(jnp.int32), axis=0, keepdims=True)
    last = jnp.where(some > 0, upto - 1, slots)
    return order, keep, last


def recompress(
    f_hbm, panel_hbm, target_hbm, count_hbm, s_hbm, c_hbm, p_hbm, left, right,
    panel, target, count, order_vec, meta, coup, cbd, fbuf, cum, pbuf, sfull, scol, coef, ysend, yrecv, zsend, zrecv, total, qall, midall,
    loc_sem, small_sem, s_send, s_recv, c_send, c_recv, g_send, g_recv, y_sem, yr_sem, z_sem, zr_sem,
    q_send, q_recv, m_send, m_recv,
):
    slots = f_hbm.shape[0]
    rank = f_hbm.shape[2]
    width = f_hbm.shape[3]
    quarter = width // NARROW
    share = width // WAYS
    w = lax.axis_index("wide")
    n = lax.axis_index("narrow")
    z, y = w // YWAY, w % YWAY
    flip = w + 1 - 2 * y

    def zflip(m):
        return (z, z + 1 - 2 * (z % 2), (z + 2) % 4, 3 - z)[m]

    def remote(src, dst, send, recv, wide_at, narrow_at):
        return pltpu.make_async_remote_copy(
            src_ref=src, dst_ref=dst, send_sem=send, recv_sem=recv,
            device_id=(wide_at, narrow_at), device_id_type=pl.DeviceIdType.MESH,
        )

    barrier = pltpu.get_barrier_semaphore()
    for k in range(1, NARROW):
        pl.semaphore_signal(
            barrier, inc=1, device_id=(w, (n + k) % NARROW), device_id_type=pl.DeviceIdType.MESH
        )
    for k in range(1, WAYS):
        pl.semaphore_signal(
            barrier, inc=1, device_id=((w + k) % WAYS, n), device_id_type=pl.DeviceIdType.MESH
        )

    smalls = [
        pltpu.make_async_copy(src, dst, small_sem.at[i])
        for i, (src, dst) in enumerate(
            ((panel_hbm, panel), (target_hbm, target), (count_hbm, count), (c_hbm, coup))
        )
    ]
    step = slots // FSPLIT
    loads = [
        pltpu.make_async_copy(
            f_hbm.at[pl.ds(i * step, step)], fbuf.at[pl.ds(i * step, step)], loc_sem.at[i]
        )
        for i in range(FSPLIT)
    ]
    own_s = pltpu.make_async_copy(s_hbm, sfull.at[n], loc_sem.at[FSPLIT])
    load_p = pltpu.make_async_copy(p_hbm, pbuf, loc_sem.at[FSPLIT + 1])
    for c in smalls:
        c.start()
    own_s.start()
    for c in loads:
        c.start()
    load_p.start()

    pl.semaphore_wait(barrier, NARROW + WAYS - 2)

    twin, across = n + 1 - 2 * (n % 2), (n + 2) % NARROW
    twin_across = (twin + 2) % NARROW
    sent = []

    def s_send_to(src, ref, sem, to):
        c = remote(src, ref, s_send.at[sem], s_recv.at[sem], w, to)
        c.start()
        sent.append(c)

    def s_wait(ref, sem):
        remote(ref, ref, s_send.at[sem], s_recv.at[sem], w, twin).wait_recv()

    for p in range(coup.shape[0]):
        s_send_to(s_hbm.at[p], sfull.at[n, p], 3 * p, across)
        s_send_to(s_hbm.at[p], sfull.at[n, p], 3 * p + 1, twin)
    for c in smalls:
        c.wait()
    order_vec[...] = jnp.zeros(order_vec.shape, jnp.int32)
    for i, row in enumerate(entry_order(panel[...], target[...], count[...], coup.shape[0])):
        order_vec[i : i + 1, :slots] = row
    meta_copy = pltpu.make_async_copy(order_vec, meta, small_sem.at[4])
    meta_copy.start()
    empty = jnp.zeros((rank, rank), jnp.float32)
    cbd[:rank] = jnp.concatenate([coup[0], empty], axis=1)
    cbd[rank:] = jnp.concatenate([empty, coup[1]], axis=1)
    for p in range(coup.shape[0]):
        s_wait(sfull.at[across, p], 3 * p)
        s_send_to(sfull.at[across, p], sfull.at[across, p], 3 * p + 2, twin)

    cum[slots] = jnp.zeros((2, rank, width), jnp.bfloat16)
    meta_copy.wait()
    for c in loads:
        c.wait()
    for c0 in range(0, rank, 16):

        def add(s, acc):
            x = fbuf[meta[0, s], 0, pl.ds(c0, 16), :].astype(jnp.float32)
            acc = acc * meta[1, s].astype(jnp.float32) + x
            high = acc.astype(jnp.bfloat16)
            cum[s, 0, pl.ds(c0, 16), :] = high
            cum[s, 1, pl.ds(c0, 16), :] = (acc - high.astype(jnp.float32)).astype(jnp.bfloat16)
            return acc

        lax.fori_loop(0, slots, add, jnp.zeros((16, width), jnp.float32), unroll=2)

    def pair_rows(t):
        first, second = meta[2, 2 * t], meta[2, 2 * t + 1]
        return jnp.concatenate(
            [cum[first, 0], cum[second, 0], cum[first, 1], cum[second, 1]], axis=0
        )

    load_p.wait()
    own_s.wait()

    def project(at):
        cols = pl.ds(pl.multiple_of(at * quarter, quarter), quarter)
        probe = pbuf[:, :, cols].reshape(-1, quarter)
        return lax.dot_general(
            probe, sfull[at].reshape(-1, quarter), LAST_DIMS, preferred_element_type=jnp.float32
        )

    projected = project(n)
    projected = projected + project(across)
    for at, sem in ((twin, 1), (twin_across, 2)):
        for p in range(coup.shape[0]):
            s_wait(sfull.at[at, p], 3 * p + sem)
        projected = projected + project(at)
    coef[...] = lax.dot_general(
        projected, cbd[...], LAST_DIMS, precision=HIGHEST, preferred_element_type=jnp.float32
    ).astype(jnp.bfloat16)

    def partial_sketch(t):
        lhs = coef[pl.ds(pl.multiple_of(t * rank, rank), rank), :]
        lhs = jnp.concatenate([lhs, lhs], axis=1)
        return jnp.dot(lhs, pair_rows(t), preferred_element_type=jnp.float32)

    order = (2, 3, 1, 0)
    cut = rank // RCUT
    y_copies, z_copies = {}, {}

    def y_stage(k):
        ysend[k] = partial_sketch(zflip(order[k]) * YWAY + (1 - y)).astype(jnp.bfloat16)
        for h in range(RCUT):
            at = pl.ds(h * cut, cut)
            c = remote(
                ysend.at[k, at], yrecv.at[k, at], y_sem.at[k, h], yr_sem.at[k, h], flip, n
            )
            c.start()
            sent.append(c)
            y_copies[k, h] = c

    def z_stage(k):
        to = zflip(order[k]) * YWAY + y
        own = partial_sketch(to)
        for h in range(RCUT):
            at = pl.ds(h * cut, cut)
            y_copies[k, h].wait_recv()
            summed = own[h * cut : (h + 1) * cut] + yrecv[k, at].astype(jnp.float32)
            if order[k]:
                zsend[k, at] = summed.astype(jnp.bfloat16)
                c = remote(
                    zsend.at[k, at], zrecv.at[k, at], z_sem.at[k, h], zr_sem.at[k, h], to, n
                )
                c.start()
                sent.append(c)
                z_copies[k, h] = c
            else:
                total[at] = summed

    y_stage(0)
    y_stage(1)
    for k in range(ZWAY):
        if k + 2 < ZWAY:
            y_stage(k + 2)
        z_stage(k)
    for k in (2, 0, 1):
        for h in range(RCUT):
            at = pl.ds(h * cut, cut)
            z_copies[k, h].wait_recv()
            total[at] += zrecv[k, at].astype(jnp.float32)

    part = rank // 2

    def s_part(to):
        cols = pl.ds(pl.multiple_of((to % 2) * share, share), share)
        rows = pl.ds(pl.multiple_of((n % 2) * part, part), part)
        return sfull.at[to // 2, n // 2, rows, cols]

    for k in range(1, WAYS):
        to = (w + k) % WAYS
        c = remote(s_part(to), scol.at[n, w], c_send.at[k], c_recv.at[k], to, n)
        c.start()
        sent.append(c)
    scol[n, w] = s_part(w)[...]

    sketch = total[...]
    gram = lax.dot_general(
        sketch, sketch, LAST_DIMS, precision=HIGHEST, preferred_element_type=jnp.float32
    )
    inverse = eliminate(gram)
    qall[w] = jnp.dot(
        inverse, sketch, precision=HIGHEST, preferred_element_type=jnp.float32
    ).astype(jnp.bfloat16)

    def middle(t):
        terms = lax.dot_general(
            qall[t], pair_rows(t), LAST_DIMS, preferred_element_type=jnp.float32
        )
        terms = terms[:, : 2 * rank] + terms[:, 2 * rank :]
        rows = jnp.dot(terms, cbd[...], precision=HIGHEST, preferred_element_type=jnp.float32)
        midall[w, pl.ds(pl.multiple_of(t * rank, rank), rank), :] = rows.astype(jnp.bfloat16)

    def arrivals(at):
        return (at, at + 1 - 2 * (at % 2), 2 - at // 2, 3 - 3 * (at // 2))

    inner = z % 3 != 0
    later = []

    def start(c, holds=None):
        if holds is None:
            c.start()
        else:
            pl.when(holds)(c.start)
        later.append((c, holds))

    def spread(ref, send, recv):
        start(remote(ref, ref, send(0), recv(ZWAY + z), flip, n))
        start(remote(ref, ref, send(1), recv(z), (z + 1) % 4 * YWAY + y, n), z < ZWAY - 1)
        start(remote(ref, ref, send(2), recv(z), (z + 3) % 4 * YWAY + y, n), z > 0)

    def pass_on(ref, j, src_z, send, recv, line=True):
        remote(ref, ref, send(0), recv(src_z), w, n).wait_recv()
        start(remote(ref, ref, send(2 + 2 * j), recv(ZWAY + src_z), flip, n))
        if line:
            to = (3 - z if j == 1 else (3 * z + 1) % 4) * YWAY + y
            start(remote(ref, ref, send(1 + 2 * j), recv(src_z), to, n), inner)

    def spread_straight(ref, send, recv, all_y):
        start(remote(ref, ref, send(0), recv(ZWAY + z), flip, n))
        for k, src_z in enumerate(arrivals(z)):
            if k:
                start(remote(ref, ref, send(k), recv(z), src_z * YWAY + y, n))
        for k, src_z in enumerate(arrivals(z)):
            if k and all_y:
                to = src_z * YWAY + 1 - y
                start(remote(ref, ref, send(3 + k), recv(ZWAY + z), to, n))

    def take(ref, src_z, send, recv):
        remote(ref, ref, send(0), recv(ZWAY + src_z), w, n).wait_recv()

    def q_sems(h):
        return (lambda k: q_send.at[h, k]), (lambda k: q_recv.at[h, k])

    def q_piece(at, h):
        return qall.at[at, pl.ds(h * (rank // QCUT), rank // QCUT), :]

    def mid_sems(i):
        return (lambda k: m_send.at[i, k]), (lambda k: m_recv.at[i, k])

    def mid_piece(src_z, src_y, i):
        first = arrivals(src_z)[i] * YWAY * rank
        rows = pl.ds(pl.multiple_of(first, YWAY * rank), YWAY * rank)
        return midall.at[src_z * YWAY + src_y, rows, :]

    for h in range(QCUT):
        spread(q_piece(w, h), *q_sems(h))
    middle(w)
    def far_half(j):
        src_z = arrivals(z)[j]
        far = src_z * YWAY + 1 - y
        for h in range(QCUT):
            take(q_piece(far, h), src_z, *q_sems(h))
        middle(far)
        if ROUTES[j] == "L":
            spread(mid_piece(z, y, j), *mid_sems(j))
        else:
            spread_straight(mid_piece(z, y, j), *mid_sems(j), ROUTES[j] == "F")

    def row_start(i):
        piece = mid_piece(z, 1 - y, i)
        send, recv = mid_sems(i)
        take(piece, z, send, recv)
        for k, src_z in enumerate(arrivals(z)):
            if k:
                start(remote(piece, piece, send(3 + k), recv(ZWAY + z), src_z * YWAY + y, n))

    def mid_pass(i, j):
        src_z = arrivals(z)[j]
        piece = mid_piece(src_z, y, i)
        send, recv = mid_sems(i)
        if ROUTES[i] in "FS":
            remote(piece, piece, send(0), recv(src_z), w, n).wait_recv()
        else:
            pass_on(piece, j, src_z, send, recv, ROUTES[i] == "L")

    for j in range(1, ZWAY):
        src_z = arrivals(z)[j]
        near = src_z * YWAY + y
        for h in range(QCUT):
            pass_on(q_piece(near, h), j, src_z, *q_sems(h))
        far_half(j - 1)
        middle(near)
    for k in range(1, WAYS):
        src = scol.at[n, (w + WAYS - k) % WAYS]
        remote(src, src, c_send.at[k], c_recv.at[k], w, twin).wait_recv()
    for k in range(1, NARROW):
        c = remote(
            scol.at[n], scol.at[n], g_send.at[k], g_recv.at[k], w, (n + k) % NARROW
        )
        c.start()
        sent.append(c)

    if ROUTES[0] == "S":
        row_start(0)
    mid_pass(0, 1)
    if ROUTES[1] == "S":
        row_start(1)
    far_half(ZWAY - 1)
    if ROUTES[2] == "S":
        row_start(2)
    for i in range(ZWAY):
        for j in range(1, ZWAY):
            if i or j > 1:
                mid_pass(i, j)

    for k in range(WAYS):
        cols = pl.ds(pl.multiple_of(w * share, share), share)
        left[k] = qall[k, :, cols]

    def rows_of(src):
        shared = jnp.concatenate([scol[k, src] for k in range(NARROW)], axis=0)
        return jnp.dot(midall[src], shared, preferred_element_type=jnp.float32)

    for k in range(1, NARROW):
        src = scol.at[(n + NARROW - k) % NARROW]
        remote(src, src, g_send.at[k], g_recv.at[k], w, twin).wait_recv()
    rows = rows_of(w)
    for j, src_z in enumerate(arrivals(z)):
        if j:
            rows = rows + rows_of(src_z * YWAY + y)
    for j, src_z in enumerate(arrivals(z)):
        for i in range(ZWAY):
            if ROUTES[i] != "S" or j:
                take(mid_piece(src_z, 1 - y, i), src_z, *mid_sems(i))
        rows = rows + rows_of(src_z * YWAY + 1 - y)
    right[...] = rows.reshape(right.shape)
    for c in sent:
        c.wait_send()
    for c, holds in later:
        if holds is None:
            c.wait_send()
        else:
            pl.when(holds)(c.wait_send)


def fused(entry_factor, entry_panel, entry_target, entry_count, panel_shared, coupling, probes):
    slots, _, rank, width = entry_factor.shape
    panels = panel_shared.shape[0]
    targets = probes.shape[0]
    share = width // WAYS
    depth = panels * rank
    bf16, f32, i32 = jnp.bfloat16, jnp.float32, jnp.int32
    dma = pltpu.SemaphoreType.DMA
    left, right = pl.pallas_call(
        recompress,
        out_shape=(
            jax.ShapeDtypeStruct((targets, rank, share), bf16),
            jax.ShapeDtypeStruct((targets, rank, share), f32),
        ),
        in_specs=[pl.BlockSpec(memory_space=pltpu.HBM)] * 7,
        out_specs=(
            pl.BlockSpec(memory_space=pltpu.VMEM),
            pl.BlockSpec(memory_space=pltpu.VMEM),
        ),
        scratch_shapes=[
            pltpu.VMEM((1, slots), i32),
            pltpu.VMEM((1, slots), i32),
            pltpu.VMEM((1, 1), i32),
            pltpu.VMEM((8, 128), i32),
            pltpu.SMEM((8, 128), i32),
            pltpu.VMEM((panels, rank, rank), f32),
            pltpu.VMEM((depth, depth), f32),
            pltpu.VMEM((slots, 1, rank, width), bf16),
            pltpu.VMEM((slots + 1, 2, rank, width), bf16),
            pltpu.VMEM((targets, rank, width), bf16),
            pltpu.VMEM((NARROW, panels, rank, width // NARROW), bf16),
            pltpu.VMEM((NARROW, WAYS, depth // NARROW, share), bf16),
            pltpu.VMEM((targets * rank, depth), bf16),
            pltpu.VMEM((ZWAY, rank, width), bf16),
            pltpu.VMEM((ZWAY, rank, width), bf16),
            pltpu.VMEM((ZWAY - 1, rank, width), bf16),
            pltpu.VMEM((ZWAY - 1, rank, width), bf16),
            pltpu.VMEM((rank, width), f32),
            pltpu.VMEM((targets, rank, width), bf16),
            pltpu.VMEM((WAYS, targets * rank, depth), bf16),
            dma((FSPLIT + 2,)),
            dma((5,)),
            dma((3 * panels,)),
            dma((3 * panels,)),
            dma((WAYS,)),
            dma((WAYS,)),
            dma((NARROW,)),
            dma((NARROW,)),
            dma((ZWAY, RCUT)),
            dma((ZWAY, RCUT)),
            dma((ZWAY, RCUT)),
            dma((ZWAY, RCUT)),
            dma((QCUT, 9)),
            dma((QCUT, WAYS)),
            dma((ZWAY, 9)),
            dma((ZWAY, WAYS)),
        ],
        compiler_params=pltpu.CompilerParams(
            collective_id=0, has_side_effects=True, vmem_limit_bytes=63 * 1024 * 1024
        ),
        name="recompress",
    )(entry_factor, entry_panel.T, entry_target.T, entry_count, panel_shared, coupling, probes)
    root_width = math.sqrt(width)
    return (left.astype(f32) * root_width, right / root_width)


def solution(mesh):
    placed = (
        P("wide", "narrow", None, None),
        P("wide", "narrow"),
        P("wide", "narrow"),
        P("narrow", "wide"),
        P("wide", None, "narrow"),
        P("wide", None, None),
        P("narrow", None, None),
    )
    return jax.shard_map(
        fused if mesh.shape["wide"] == WAYS and mesh.shape["narrow"] == NARROW else shards,
        mesh=mesh,
        in_specs=placed,
        out_specs=(P("narrow", None, "wide"), P("narrow", None, "wide")),
        check_vma=False,
    )
```
